256 devices in a mesh: lat: 16 (over z_lo, x, core), lon: 4 (over y), bin: 4 (over z_hi).
Axes of the slice: x: 4, y: 4, z: 8 (z_hi: 4, z_lo: 2; z = z_hi * 2 + z_lo), core: 2. Of those that a mesh axis runs over, the one named last changes fastest.
Arguments:
- inputs: bfloat16 [512, 1024, 128], P(('lat', 'bin'), 'lon'), may hold values from -70 to 70
- conv_one: bfloat16 [3, 3, 128, 128], replicated, may hold values from -0.1875 to 0.1875
- conv_two: bfloat16 [3, 3, 128, 128], replicated, may hold values from -0.1875 to 0.1875
- head_weight: bfloat16 [4, 128, 512], P(None, None, 'bin'), may hold values from -45.078057 to 45.078057
- targets: int32 [4, 512, 1024], P(None, 'lat', 'lon'), may hold values from 0 to 511
Outputs:
- loss_mean: float32 [], replicated
- grad_conv_one: float32 [3, 3, 128, 128], replicated
- grad_conv_two: float32 [3, 3, 128, 128], replicated
- grad_heads: float32 [4, 128, 512], P(None, None, 'bin')
The draws below stay inside these ranges and needn't reach their ends.
All inputs are finite; a program needn't handle non-finite values.
Results may differ from the reference program's by a relative error of at most 0.0035.
The reference program's roundings to bfloat16 on the way (of `act_one`, `act_two`, `logit_grad`, `back_two` and `back_one`) count: a program that leaves them out, or rounds other values in their place, can miss the bound.
Values may be sent and summed in bfloat16 or wider, within the bound.
A program may use at most 64 MiB of HBM per device.

```python
import math
import jax
import jax.numpy as jnp
from jax import lax

C = 128
BINS = 512
HEADS = 4
NX = 512
NY = 1024


def draw_inputs(key, part):
    first, second, third = jax.random.split(key, 3)
    normal = jnp.clip(jax.random.normal(first, (NX, NY, C), jnp.float32), -5.0, 5.0)
    cellwise = jax.random.uniform(second, (NX, NY, 1), jnp.float32, 0.6, 1.4)
    channel_scale = jnp.exp(jax.random.uniform(third, (1, 1, C), jnp.float32, -0.7, 0.7))
    rising = 3.0 ** (jnp.arange(NX, dtype=jnp.float32) / NX)
    result = normal * rising.reshape(NX, 1, 1) * cellwise * channel_scale
    return result.astype(jnp.bfloat16)


def draw_head_weight(key, part):
    first = jax.random.fold_in(key, 0)
    normal = jnp.clip(jax.random.normal(first, (HEADS, C, BINS), jnp.float32), -5.0, 5.0)
    spread = 4.0 / math.sqrt(C)
    return (normal * spread).astype(jnp.bfloat16)


def place_ends(values, rng, smallest, largest):
    longest = values.shape.index(max(values.shape))
    spots = []
    for shift in (0, 1):
        where = [jax.random.randint(jax.random.fold_in(rng, axis), (), 0, length) for axis, length in enumerate(values.shape)]
        where[longest] = (where[longest] + shift) % values.shape[longest]
        spots.append(tuple(where))
    return values.at[spots[0]].set(smallest).at[spots[1]].set(largest)


def gaussian(stream_key, extent, scale, limit, held_as=jnp.bfloat16):
    drawn = jax.random.normal(stream_key, extent, jnp.float32) * scale
    return jnp.minimum(jnp.maximum(drawn, -limit), limit).astype(held_as)


def setup_inputs(seed: int = 0) -> dict:
    arg_keys = jax.random.split(jax.random.key(seed), 6)
    inputs = draw_inputs(jax.random.fold_in(arg_keys[5], 71), 0)
    conv_one = gaussian(arg_keys[1], (3, 3, C, C), (9 * C) ** -0.5, 0.1875)
    conv_two = gaussian(arg_keys[2], (3, 3, C, C), (9 * C) ** -0.5, 0.1875)
    head_weight = draw_head_weight(jax.random.fold_in(arg_keys[5], 71), 0)
    targets = place_ends(jax.random.randint(arg_keys[4], (HEADS, NX, NY), 0, BINS), jax.random.fold_in(arg_keys[4], 1), 0, BINS - 1).astype(jnp.int32)
    return dict(inputs=inputs, conv_one=conv_one, conv_two=conv_two, head_weight=head_weight, targets=targets)


def shifted_product(padded, kernel, grid_rows, grid_cols):
    total = jnp.zeros((grid_rows * grid_cols, kernel.shape[-1]), jnp.float32)
    for a in range(3):
        for b in range(3):
            window = padded[a:a + grid_rows, b:b + grid_cols].reshape(grid_rows * grid_cols, -1)
            total = total + jnp.dot(window, kernel[a, b], preferred_element_type=jnp.float32)
    return total

def kernel_grad(padded, upstream, grid_rows, grid_cols):
    result = []
    for a in range(3):
        for b in range(3):
            window = padded[a:a + grid_rows, b:b + grid_cols].reshape(grid_rows * grid_cols, -1)
            result.append(jnp.dot(window.T, upstream, preferred_element_type=jnp.float32))
    channels = upstream.shape[1]
    return jnp.stack(result).reshape(3, 3, window.shape[1], channels)

def border(values_in):
    return jnp.pad(values_in, ((1, 1), (1, 1), (0, 0)))

def reference(inputs, conv_one, conv_two, head_weight, targets):
    channels = C
    padded_in = border(inputs)
    pre_one = shifted_product(padded_in, conv_one, NX, NY)
    act_one = jnp.maximum(pre_one, 0.0).astype(jnp.bfloat16)
    padded_one = border(act_one.reshape(NX, NY, channels))
    pre_two = shifted_product(padded_one, conv_two, NX, NY)
    act_two = jnp.maximum(pre_two, 0.0).astype(jnp.bfloat16)
    loss_scale = 1.0 / math.sqrt(HEADS * NX * NY)
    cell_count = NX * NY
    block_rows = math.gcd(cell_count, 16384)
    block_count = cell_count // block_rows
    feat_blocks = act_two.reshape(block_count, block_rows, channels)
    label_blocks = targets.reshape(HEADS, block_count, block_rows).transpose(1, 0, 2)
    columns = jnp.arange(BINS, dtype=jnp.int32)[None, :]

    def step(carry, inputs_now):
        loss_sum, gradients = carry
        feat_rows, label_rows = inputs_now
        hidden_back = jnp.zeros((block_rows, channels), jnp.float32)
        for k in range(HEADS):
            logits = jnp.dot(feat_rows, head_weight[k], preferred_element_type=jnp.float32)
            log_total = jax.nn.logsumexp(logits, axis=1)
            chosen = columns == label_rows[k][:, None]
            picked = lax.optimization_barrier(jnp.sum(jnp.where(chosen, logits, 0.0), axis=1))
            loss_sum = loss_sum + jnp.sum(log_total - picked)
            logit_grad = ((jnp.exp(logits - log_total[:, None]) - jnp.where(chosen, 1.0, 0.0)) * loss_scale).astype(jnp.bfloat16)
            gradients = gradients.at[k].add(jnp.dot(feat_rows.T, logit_grad, preferred_element_type=jnp.float32))
            hidden_back = hidden_back + jnp.dot(logit_grad, head_weight[k].T, preferred_element_type=jnp.float32)
        return ((loss_sum, gradients), hidden_back)
    start = (jnp.zeros((), jnp.float32), jnp.zeros((HEADS, channels, BINS), jnp.float32))
    (loss_sum, grad_heads), backs = lax.scan(step, start, (feat_blocks, label_blocks))
    hidden_back = backs.reshape(cell_count, channels)
    back_two = jnp.where(pre_two > 0, hidden_back, 0.0).astype(jnp.bfloat16)
    grad_conv_two = kernel_grad(padded_one, back_two, NX, NY)
    flipped = conv_two[::-1, ::-1].transpose(0, 1, 3, 2)
    back_act = shifted_product(border(back_two.reshape(NX, NY, channels)), flipped, NX, NY)
    back_one = jnp.where(pre_one > 0, back_act, 0.0).astype(jnp.bfloat16)
    grad_conv_one = kernel_grad(padded_in, back_one, NX, NY)
    loss_mean = loss_sum / (HEADS * NX * NY)
    return (loss_mean, grad_conv_one, grad_conv_two, grad_heads)
```

```python
import functools
import math

import jax
import jax.numpy as jnp
from jax import lax
from jax.experimental import pallas as pl
from jax.experimental.pallas import tpu as pltpu
from jax.sharding import PartitionSpec as P

BF = jnp.bfloat16
F32 = jnp.float32
MESH = pl.DeviceIdType.MESH
CORES = 2
PLANE_X = 4


def dot(left, right, contract=((1,), (0,))):
    return lax.dot_general(left, right, (contract, ((), ())), preferred_element_type=F32)


def layout(lat, lon, bins):
    plane_x = min(PLANE_X, lat // CORES)
    return dict(nx=plane_x, nzl=lat // (CORES * plane_x), ny=lon, nzh=bins)


def plan(lat, lon, bins, rows, width, channels, heads, bin_width):
    d = layout(lat, lon, bins)
    nq, nz = d["nx"] * d["ny"], d["nzl"] * d["nzh"]
    qr = channels // nq
    pitch = width + 16
    total = bins * bin_width
    vm, dma = pltpu.VMEM, pltpu.SemaphoreType.DMA
    s = dict(
        frame=vm(((rows + 2) * pitch, channels), F32),
        px=vm(((rows + 2) * width, 3 * channels), BF),
        pa=vm(((rows + 2) * width, 3 * channels), BF),
        pg=vm(((rows + 2) * width, 3 * channels), BF),
        w_one=vm((12 * channels, 2 * channels), BF),
        w_two=vm((12 * channels, 2 * channels), BF),
        w_flip=vm((12 * channels, 2 * channels), BF),
        act_one=vm((rows, width, channels), BF),
        act_two=vm((rows, width, channels), BF),
        back_two=vm((rows + 2, width, channels), BF),
        back_one=vm((rows + 2, width, channels), BF),
        pre_one=vm((rows, width, channels), F32),
        pre_two=vm((rows, width, channels), F32),
        hw_all=vm((bins, heads, channels, bin_width), BF),
        hw_rows=vm((heads, total, channels), BF),
        hw_cols=vm((heads, channels, total), BF),
        gh_acc=vm((heads, total, channels), F32),
        loss_acc=vm((1, width), F32),
        g_acc=vm((3 * channels, 3 * channels), F32),
        col_out=vm((3, 2, rows, channels), F32),
        col_in=vm((3, 2, 3, rows, channels), F32),
        row_in=vm((3, 2, width, channels), BF),
        halo_send=dma((3, 8)),
        halo_recv=dma((3, 8)),
        hw_send=dma((2, bins)),
        hw_recv=dma((2, bins)),
    )
    shapes = dict(gh=((bins, heads // 2), (heads // 2,)), g2=((5,), (5,)), g1=((5,), (5,)))
    for name, (first, second) in shapes.items():
        tile = (qr, channels)
        s[name + "_part"] = vm((2, nq) + first + tile, BF)
        s[name + "_core"] = vm((nq,) + first + tile, BF)
        s[name + "_half"] = vm((nq,) + first + tile, BF)
        s[name + "_plane"] = vm((nq,) + first + tile, BF)
        s[name + "_sum"] = vm(first + tile, BF)
        s[name + "_ring"] = vm((nz,) + second + tile, BF)
        s[name + "_out"] = vm((2, nq) + second + tile, BF)
        s[name + "_send"] = dma((2 + 2 * nq + nz,))
        s[name + "_recv"] = dma((2 + 2 * nq + nz,))
    return s


class Place:
    def __init__(self, lat, lon, bins):
        self.__dict__.update(layout(lat, lon, bins))
        self.lat_size, self.lon_size, self.bin_size = lat, lon, bins
        self.lat, self.lon, self.bin = (lax.axis_index(a) for a in ("lat", "lon", "bin"))
        self.core = self.lat % CORES
        self.x = (self.lat // CORES) % self.nx
        self.zlo = self.lat // (CORES * self.nx)
        self.y = self.lon
        self.nq, self.nz = self.nx * self.ny, self.nzl * self.nzh
        self.z = self.bin * self.nzl + self.zlo
        self.q = self.x * self.ny + self.y
        self.row_block = self.lat * bins + self.bin
        self.row_blocks = lat * bins

    def device(self, lat=None, lon=None, bin=None):
        pick = lambda v, own: own if v is None else v
        return dict(lat=pick(lat, self.lat), lon=pick(lon, self.lon), bin=pick(bin, self.bin))

    def at(self, core=None, x=None, zlo=None):
        core = self.core if core is None else core
        x = self.x if x is None else x
        zlo = self.zlo if zlo is None else zlo
        return (zlo * self.nx + x) * CORES + core

    def partner(self):
        return self.device(lat=self.at(core=1 - self.core))

    def plane(self):
        for dx in range(self.nx):
            for dy in range(self.ny):
                if dx or dy:
                    x, y = (self.x + dx) % self.nx, (self.y + dy) % self.ny
                    yield dx * self.ny + dy, x * self.ny + y, self.device(lat=self.at(x=x), lon=y)

    def ring(self):
        for dz in range(1, self.nz):
            z = (self.z + dz) % self.nz
            zhi, zlo = z // self.nzl, z % self.nzl
            yield dz, zhi, self.device(lat=self.at(zlo=zlo), bin=zhi)

    def bins(self):
        for db in range(1, self.bin_size):
            yield db, self.device(bin=(self.bin + db) % self.bin_size)

    def neighbour(self, down, right):
        block = (self.row_block + down) % self.row_blocks
        return self.device(
            lat=block // self.bin_size, lon=(self.lon + right) % self.lon_size, bin=block % self.bin_size
        )


NEIGHBOURS = [(-1, 0), (1, 0), (0, -1), (0, 1), (-1, -1), (-1, 1), (1, -1), (1, 1)]


def enter(place):
    barrier = pltpu.get_barrier_semaphore()
    peers = [place.neighbour(*n) for n in NEIGHBOURS]
    peers += [place.partner()]
    peers += [device for _, _, device in place.plane()]
    peers += [device for _, _, device in place.ring()]
    for device in peers:
        pl.semaphore_signal(barrier, inc=1, device_id=device, device_id_type=MESH)
    pl.semaphore_wait(barrier, len(peers))


def remote(src, dst, send, recv, device):
    copy = pltpu.make_async_remote_copy(
        src_ref=src, dst_ref=dst, send_sem=send, recv_sem=recv, device_id=device, device_id_type=MESH
    )
    copy.start()
    return copy


class Halo:
    def __init__(self, k, place, s):
        self.k, self.place, self.s = k, place, s
        self.rows, self.width, _ = s["act_one"].shape
        self.pitch = self.width + 16

    def line(self, r):
        return pl.ds((r + 1) * self.pitch + 8, self.width)

    def column(self, c):
        return pl.ds(self.pitch + 8 + c, self.rows, stride=self.pitch)

    def send(self, rows_ref, top, bottom):
        k, place, s, frame = self.k, self.place, self.s, self.s["frame"]
        self.copies = []

        def go(i, src, dst, down, right):
            self.copies.append(
                remote(src, dst, s["halo_send"].at[k, i], s["halo_recv"].at[k, i], place.neighbour(down, right))
            )

        go(0, rows_ref.at[top], s["row_in"].at[k, 1], -1, 0)
        go(1, rows_ref.at[bottom], s["row_in"].at[k, 0], 1, 0)
        s["col_out"][k, 0] = frame[self.column(0), :]
        s["col_out"][k, 1] = frame[self.column(self.width - 1), :]
        for i, (down, right) in list(enumerate(NEIGHBOURS))[2:]:
            src = s["col_out"].at[k, 0 if right < 0 else 1]
            dst = s["col_in"].at[k, 1 if right < 0 else 0, 1 - down]
            go(i, src, dst, down, right)

    def receive(self):
        k, place, s, frame = self.k, self.place, self.s, self.s["frame"]
        for copy in self.copies:
            copy.wait()
        up = place.row_block > 0
        down = place.row_block < place.row_blocks - 1
        left = place.lon > 0
        right = place.lon < place.lon_size - 1
        rows, width, pitch = self.rows, self.width, self.pitch
        frame[self.line(-1), :] = jnp.where(up, s["row_in"][k, 0].astype(F32), 0.0)
        frame[self.line(rows), :] = jnp.where(down, s["row_in"][k, 1].astype(F32), 0.0)
        for side, there, c in ((0, left, -1), (1, right, width)):
            got = s["col_in"]
            frame[self.column(c), :] = jnp.where(there, got[k, side, 1], 0.0)
            frame[pl.ds(8 + c, 1), :] = jnp.where(
                there & up, got[k, side, 0, pl.ds(rows - 1, 1), :], 0.0
            )
            frame[pl.ds((rows + 1) * pitch + 8 + c, 1), :] = jnp.where(
                there & down, got[k, side, 2, pl.ds(0, 1), :], 0.0
            )


def fill_patches(frame, patches, rows, width):
    pitch = width + 16

    def body(r, carry):
        to = pl.multiple_of(r * width, width)
        for b in range(3):
            window = frame[pl.ds(r * pitch + 7 + b, width), :]
            patches[pl.ds(to, width), b * 128 : (b + 1) * 128] = window.astype(BF)
        return carry

    lax.fori_loop(0, rows + 2, body, 0)


def fill_weights(out, taps, channels):
    wide = 3 * channels
    out[pl.ds(3 * wide, wide), :channels] = jnp.zeros((wide, channels), BF)
    out[pl.ds(0, wide), channels:] = jnp.zeros((wide, channels), BF)
    for a in range(3):
        for b in range(3):
            tap = taps(a, b)
            for second in range(2):
                at = (a + second) * wide + b * channels
                out[at : at + channels, second * channels : (second + 1) * channels] = tap


def convolve(patches, weights, rows, width, finish):
    def body(p, carry):
        lines = [
            patches[pl.ds(pl.multiple_of((2 * p + a) * width, width), width), :] for a in range(4)
        ]
        both = dot(jnp.concatenate(lines, axis=1), weights[...])
        half = both.shape[1] // 2
        finish(2 * p, both[:, :half])
        finish(2 * p + 1, both[:, half:])
        return carry

    lax.fori_loop(0, rows // 2, body, 0)


def kernel_grad(patches, upstream, acc, rows, width):
    channels = upstream.shape[2]
    upstream[0] = jnp.zeros((width, channels), BF)
    upstream[rows + 1] = jnp.zeros((width, channels), BF)
    group = rows // 2
    for g in range(2):
        left = patches[pl.ds((1 + g * group) * width, group * width), :]
        right = jnp.concatenate(
            [
                jnp.concatenate([upstream[1 + g * group + r + 1 - a] for a in range(3)], axis=1)
                for r in range(group)
            ],
            axis=0,
        )
        value = dot(left, right, ((0,), (0,)))
        if g == 0:
            acc[...] = value
        else:
            acc[...] += value
    acc[:, :channels] += dot(patches[pl.ds(0, width), :], upstream[1], ((0,), (0,)))
    acc[:, 2 * channels :] += dot(
        patches[pl.ds((rows + 1) * width, width), :], upstream[rows], ((0,), (0,))
    )


def joined(tile):
    total = jnp.sum(tile, axis=0, keepdims=True)
    high = total.astype(BF).astype(F32)
    row = lax.broadcasted_iota(jnp.int32, tile.shape, 0)
    return jnp.where(row == 0, high, jnp.where(row == 1, total - high, 0.0))


class Reduce:
    def __init__(self, name, place, s, spread, extra=False):
        self.place, self.spread, self.extra = place, spread, extra
        for part in ("part", "core", "half", "plane", "sum", "ring", "out", "send", "recv"):
            setattr(self, part, s[name + "_" + part])
        self.sems = 0

    def go(self, src, dst, i, device):
        return remote(src, dst, self.send.at[i], self.recv.at[i], device)

    def rounded(self, value):
        if not self.extra:
            return value.astype(BF)
        last = jnp.where(self.place.core == 1, joined(value[4]), value[4])
        return jnp.concatenate([value[:4], last[None]], axis=0).astype(BF)

    def step0(self):
        p = self.place
        self.copies = [self.go(self.part.at[1 - p.core], self.core, 0, p.partner())]

    def step1(self):
        p = self.place
        for copy in self.copies:
            copy.wait()

        def body(i, carry):
            value = self.part[p.core, i].astype(F32) + self.core[i].astype(F32)
            self.half[i] = self.rounded(value)
            return carry

        lax.fori_loop(0, p.nq, body, 0)
        self.copies = [
            self.go(self.half.at[q], self.plane.at[d], 1 + d, device) for d, q, device in p.plane()
        ]

    def step2(self):
        p = self.place
        for copy in self.copies:
            copy.wait()
        value = self.half[p.q].astype(F32)
        for d in range(1, p.nq):
            value = value + self.plane[d].astype(F32)
        self.sum[...] = self.rounded(value)
        if self.spread:
            self.ring[p.z] = self.sum[p.bin]
        else:
            self.ring[p.z] = self.sum[...]
        self.copies = [
            self.go(self.sum.at[zhi] if self.spread else self.sum, self.ring.at[p.z], 1 + p.nq + dz, device)
            for dz, zhi, device in p.ring()
        ]

    def step3(self):
        p = self.place
        for copy in self.copies:
            copy.wait()
        value = self.ring[0].astype(F32)
        for z in range(1, p.nz):
            value = value + self.ring[z].astype(F32)
        self.out[p.core, p.q] = self.rounded(value)
        mine = self.out.at[p.core, p.q]
        base = 1 + p.nq + p.nz
        self.copies = [self.go(mine, mine, base + d, device) for d, _, device in p.plane()]

    def step4(self):
        p = self.place
        for copy in self.copies:
            copy.wait()
        mine = self.out.at[p.core]
        self.copies = [self.go(mine, mine, 1 + 2 * p.nq + p.nz, p.partner())]

    def step5(self):
        for copy in self.copies:
            copy.wait()


def pack_grad(acc, part, channels):
    qr = part.shape[-2]
    for a in range(3):
        for b in range(3):
            c, t = divmod(3 * a + b, 5)
            tap = acc[b * channels : (b + 1) * channels, a * channels : (a + 1) * channels]
            part[c, :, t] = tap.reshape(channels // qr, qr, channels).astype(BF)


def unpack_grad(out, result, channels):
    for a in range(3):
        for b in range(3):
            c, t = divmod(3 * a + b, 5)
            result[a, b] = out[c, :, t].astype(F32).reshape(channels, channels)


def turned(tile):
    return jnp.transpose(tile.astype(F32)).astype(BF)


def kernel(sizes, names, x_ref, w1_ref, w2_ref, hw_ref, tg_ref, loss_ref, g1_ref, g2_ref, gh_ref, *refs):
    lat, lon, bins, cells_all = sizes
    s = dict(zip(names, refs))
    place = Place(lat, lon, bins)
    rows, width, channels = x_ref.shape
    heads, total = s["gh_acc"].shape[:2]
    bin_width = total // bins
    frame = s["frame"]
    scale = 1.0 / math.sqrt(heads * cells_all)

    enter(place)

    halo = Halo(0, place, s)
    for r in range(rows):
        frame[halo.line(r), :] = x_ref[r].astype(F32)
    halo.send(x_ref, 0, rows - 1)

    hw_all = s["hw_all"]
    half_heads = heads // 2
    my_heads = pl.ds(place.core * half_heads, half_heads)
    hw_copies = [
        remote(
            hw_ref.at[my_heads],
            hw_all.at[place.bin, my_heads],
            s["hw_send"].at[0, db],
            s["hw_recv"].at[0, db],
            device,
        )
        for db, device in place.bins()
    ]
    hw_all[place.bin] = hw_ref[...]
    fill_weights(s["w_one"], lambda a, b: w1_ref[a, b], channels)
    fill_weights(s["w_two"], lambda a, b: w2_ref[a, b], channels)
    fill_weights(s["w_flip"], lambda a, b: turned(w2_ref[2 - a, 2 - b]), channels)

    halo.receive()
    fill_patches(frame, s["px"], rows, width)

    def finish_one(r, value):
        s["pre_one"][r] = value
        act = jnp.maximum(value, 0.0).astype(BF)
        s["act_one"][r] = act
        frame[pl.ds(pl.multiple_of((r + 1) * halo.pitch + 8, 8), width), :] = act.astype(F32)

    convolve(s["px"], s["w_one"], rows, width, finish_one)
    halo = Halo(1, place, s)
    halo.send(s["act_one"], 0, rows - 1)

    for copy in hw_copies:
        copy.wait()
    hw_copies = []
    for db in range(1, bins):
        there = hw_all.at[(place.bin + db) % bins, my_heads]
        hw_copies.append(
            remote(there, there, s["hw_send"].at[1, db], s["hw_recv"].at[1, db], place.partner())
        )

    halo.receive()
    fill_patches(frame, s["pa"], rows, width)

    def finish_two(r, value):
        s["pre_two"][r] = value
        s["act_two"][r] = jnp.maximum(value, 0.0).astype(BF)

    convolve(s["pa"], s["w_two"], rows, width, finish_two)

    for copy in hw_copies:
        copy.wait()
    hw_rows, hw_cols, gh_acc = s["hw_rows"], s["hw_cols"], s["gh_acc"]
    for b in range(bins):
        for k in range(heads):
            tile = hw_all[b, k]
            hw_cols[k, :, b * bin_width : (b + 1) * bin_width] = tile
            hw_rows[k, b * bin_width : (b + 1) * bin_width, :] = turned(tile)
    gh_acc[...] = jnp.zeros_like(gh_acc)
    s["loss_acc"][...] = jnp.zeros_like(s["loss_acc"])
    first_row = place.bin * rows

    def heads_body(r, carry):
        feat = s["act_two"][r]
        feat_t = turned(feat)
        back = jnp.zeros((channels, width), F32)
        loss = s["loss_acc"][...]
        for k in range(heads):
            logits = dot(hw_rows[k], feat_t)
            highest = jnp.max(logits, axis=0, keepdims=True)
            raised = jnp.exp(logits - highest)
            summed = jnp.sum(raised, axis=0, keepdims=True)
            label = tg_ref[k, pl.ds(first_row + r, 1), :]
            chosen = lax.broadcasted_iota(jnp.int32, logits.shape, 0) == label
            picked = jnp.sum(jnp.where(chosen, logits, 0.0), axis=0, keepdims=True)
            loss = loss + (highest + jnp.log(summed) - picked)
            grad = (raised * (scale / summed) - jnp.where(chosen, scale, 0.0)).astype(BF)
            gh_acc[k] += dot(grad, feat)
            back = back + dot(hw_cols[k], grad)
        s["loss_acc"][...] = loss
        hidden = jnp.where(s["pre_two"][r] > 0, jnp.transpose(back), 0.0)
        s["back_two"][r + 1] = hidden.astype(BF)
        frame[pl.ds(pl.multiple_of((r + 1) * halo.pitch + 8, 8), width), :] = hidden.astype(BF).astype(F32)
        return carry

    lax.fori_loop(0, rows, heads_body, 0)
    halo = Halo(2, place, s)
    halo.send(s["back_two"], 1, rows)

    gh = Reduce("gh", place, s, True)
    g2 = Reduce("g2", place, s, False, extra=True)
    g1 = Reduce("g1", place, s, False)
    qr = gh.part.shape[-2]
    for k in range(heads):
        c, kk = divmod(k, half_heads)
        for b in range(bins):
            block = gh_acc[k, b * bin_width : (b + 1) * bin_width, :]
            gh.part[c, :, b, kk] = block.reshape(bin_width // qr, qr, channels).astype(BF)
    gh.step0()

    kernel_grad(s["pa"], s["back_two"], s["g_acc"], rows, width)
    pack_grad(s["g_acc"], g2.part, channels)
    loss = s["loss_acc"][...]
    lanes = loss[:, :128]
    for i in range(1, width // 128):
        lanes = lanes + loss[:, i * 128 : (i + 1) * 128]
    row = lax.broadcasted_iota(jnp.int32, (qr, 128), 0)
    loss_tile = joined(jnp.where(row == 0, lanes, 0.0)).astype(BF)
    for q in range(place.nq):
        g2.part[1, q, 4] = loss_tile
        g1.part[1, q, 4] = jnp.zeros((qr, channels), BF)
    g2.step0()

    halo.receive()
    fill_patches(frame, s["pg"], rows, width)
    gh.step1()

    def finish_back(r, value):
        s["back_one"][r + 1] = jnp.where(s["pre_one"][r] > 0, value, 0.0).astype(BF)

    convolve(s["pg"], s["w_flip"], rows, width, finish_back)
    g2.step1()
    kernel_grad(s["px"], s["back_one"], s["g_acc"], rows, width)
    pack_grad(s["g_acc"], g1.part, channels)
    g1.step0()
    gh.step2()
    g1.step1()
    g2.step2()
    gh.step3()
    g1.step2()
    g2.step3()
    g1.step3()
    gh.step4()
    g2.step4()
    gh.step5()
    for k in range(heads):
        c, kk = divmod(k, half_heads)
        gh_ref[k] = jnp.transpose(gh.out[c, :, kk].astype(F32).reshape(bin_width, channels))
    g2.step5()
    unpack_grad(g2.out, g2_ref, channels)
    whole = jnp.sum(g2.out[1, 0, 4].astype(F32), axis=0, keepdims=True)
    loss_ref[...] = jnp.sum(whole, axis=1, keepdims=True) * (1.0 / (heads * cells_all))
    g1.step4()
    g1.step5()
    unpack_grad(g1.out, g1_ref, channels)


def per_device(inputs, conv_one, conv_two, head_weight, targets):
    rows, width, channels = inputs.shape
    heads, _, bin_width = head_weight.shape
    lat, lon, bins = (lax.axis_size(a) for a in ("lat", "lon", "bin"))
    cells_all = rows * lat * bins * width * lon
    scratch = plan(lat, lon, bins, rows, width, channels, heads, bin_width)
    vmem = pl.BlockSpec(memory_space=pltpu.VMEM)
    loss, g1, g2, gh = pl.pallas_call(
        functools.partial(kernel, (lat, lon, bins, cells_all), tuple(scratch)),
        out_shape=[
            jax.ShapeDtypeStruct((1, 1), F32),
            jax.ShapeDtypeStruct(conv_one.shape, F32),
            jax.ShapeDtypeStruct(conv_two.shape, F32),
            jax.ShapeDtypeStruct(head_weight.shape, F32),
        ],
        in_specs=[vmem] * 5,
        out_specs=[vmem] * 4,
        scratch_shapes=list(scratch.values()),
        compiler_params=pltpu.CompilerParams(
            collective_id=0, has_side_effects=True, vmem_limit_bytes=56 << 20
        ),
    )(inputs, conv_one, conv_two, head_weight, targets)
    return (loss.reshape(()), g1, g2, gh)


def solution(mesh):
    in_specs = (
        P(("lat", "bin"), "lon", None),
        P(),
        P(),
        P(None, None, "bin"),
        P(None, "lat", "lon"),
    )
    out_specs = (P(), P(), P(), P(None, None, "bin"))
    return jax.shard_map(
        per_device, mesh=mesh, in_specs=in_specs, out_specs=out_specs, check_vma=False
    )
```

```python
import functools
import math

import jax
import jax.numpy as jnp
from jax import lax
from jax.experimental import pallas as pl
from jax.experimental.pallas import tpu as pltpu
from jax.sharding import PartitionSpec as P

BF = jnp.bfloat16
F32 = jnp.float32
MESH = pl.DeviceIdType.MESH
CORES = 2
PLANE_X = 4


def dot(left, right, contract=((1,), (0,))):
    return lax.dot_general(left, right, (contract, ((), ())), preferred_element_type=F32)


def layout(lat, lon, bins):
    plane_x = min(PLANE_X, lat // CORES)
    return dict(nx=plane_x, nzl=lat // (CORES * plane_x), ny=lon, nzh=bins)


def plan(lat, lon, bins, rows, width, channels, heads, bin_width):
    d = layout(lat, lon, bins)
    nq, nz = d["nx"] * d["ny"], d["nzl"] * d["nzh"]
    qr = channels // nq
    pitch = width + 16
    total = bins * bin_width
    vm, dma = pltpu.VMEM, pltpu.SemaphoreType.DMA
    s = dict(
        frame=vm(((rows + 2) * pitch, channels), F32),
        px=vm(((rows + 2) * width, 3 * channels), BF),
        pa=vm(((rows + 2) * width, 3 * channels), BF),
        pg=vm(((rows + 2) * width, 3 * channels), BF),
        w_one=vm((12 * channels, 2 * channels), BF),
        w_two=vm((12 * channels, 2 * channels), BF),
        w_flip=vm((12 * channels, 2 * channels), BF),
        act_one=vm((rows, width, channels), BF),
        act_two=vm((rows, width, channels), BF),
        back_two=vm((rows + 2, width, channels), BF),
        back_one=vm((rows + 2, width, channels), BF),
        pre_one=vm((rows, width, channels), F32),
        pre_two=vm((rows, width, channels), F32),
        hw_all=vm((bins, heads, channels, bin_width), BF),
        hw_rows=vm((heads, total, channels), BF),
        hw_cols=vm((heads, channels, total), BF),
        head_grad=vm((rows, heads, total, width), BF),
        x=vm((rows, width, channels), BF),
        w1=vm((3, 3, channels, channels), BF),
        w2=vm((3, 3, channels, channels), BF),
        tg=vm((heads, rows, width), jnp.int32),
        load=dma((5,)),
        store=dma((6,)),
        loss_acc=vm((1, width), F32),
        g_acc=vm((3 * channels, 3 * channels), F32),
        col_out=vm((3, 2, 2, rows, channels), F32),
        col_in=vm((3, 2, 3, rows, channels), F32),
        row_in=vm((3, 2, width, channels), BF),
        halo_send=dma((3, 8)),
        halo_recv=dma((3, 8)),
        hw_send=dma((2, bins)),
        hw_recv=dma((2, bins)),
    )
    shapes = dict(gh=((bins, heads // 2), (heads // 2,)), g2=((5,), (5,)), g1=((5,), (5,)))
    for name, (first, second) in shapes.items():
        tile = (qr, channels)
        s[name + "_part"] = vm((2, nq) + first + tile, BF)
        s[name + "_core"] = vm((nq,) + first + tile, BF)
        s[name + "_half"] = vm((nq,) + first + tile, BF)
        s[name + "_plane"] = vm((nq,) + first + tile, BF)
        s[name + "_sum"] = vm(first + tile, BF)
        s[name + "_ring"] = vm((nz,) + second + tile, BF)
        s[name + "_out"] = vm((2, nq) + second + tile, BF)
        s[name + "_send"] = dma((2 + 2 * nq + nz,))
        s[name + "_recv"] = dma((2 + 2 * nq + nz,))
    return s


class Place:
    def __init__(self, lat, lon, bins):
        self.__dict__.update(layout(lat, lon, bins))
        self.lat_size, self.lon_size, self.bin_size = lat, lon, bins
        self.lat, self.lon, self.bin = (lax.axis_index(a) for a in ("lat", "lon", "bin"))
        self.core = self.lat % CORES
        self.x = (self.lat // CORES) % self.nx
        self.zlo = self.lat // (CORES * self.nx)
        self.y = self.lon
        self.nq, self.nz = self.nx * self.ny, self.nzl * self.nzh
        self.z = self.bin * self.nzl + self.zlo
        self.q = self.x * self.ny + self.y
        self.row_block = self.lat * bins + self.bin
        self.row_blocks = lat * bins

    def device(self, lat=None, lon=None, bin=None):
        pick = lambda v, own: own if v is None else v
        return dict(lat=pick(lat, self.lat), lon=pick(lon, self.lon), bin=pick(bin, self.bin))

    def at(self, core=None, x=None, zlo=None):
        core = self.core if core is None else core
        x = self.x if x is None else x
        zlo = self.zlo if zlo is None else zlo
        return (zlo * self.nx + x) * CORES + core

    def partner(self):
        return self.device(lat=self.at(core=1 - self.core))

    def plane(self):
        for dx in range(self.nx):
            for dy in range(self.ny):
                if dx or dy:
                    x, y = (self.x + dx) % self.nx, (self.y + dy) % self.ny
                    yield dx * self.ny + dy, x * self.ny + y, self.device(lat=self.at(x=x), lon=y)

    def ring(self):
        for dz in range(1, self.nz):
            z = (self.z + dz) % self.nz
            zhi, zlo = z // self.nzl, z % self.nzl
            yield dz, zhi, self.device(lat=self.at(zlo=zlo), bin=zhi)

    def bins(self):
        for db in range(1, self.bin_size):
            yield db, self.device(bin=(self.bin + db) % self.bin_size)

    def neighbour(self, down, right):
        block = (self.row_block + down) % self.row_blocks
        return self.device(
            lat=block // self.bin_size, lon=(self.lon + right) % self.lon_size, bin=block % self.bin_size
        )


NEIGHBOURS = [(-1, 0), (1, 0), (0, -1), (0, 1), (-1, -1), (-1, 1), (1, -1), (1, 1)]


def enter(place):
    barrier = pltpu.get_barrier_semaphore()
    peers = [place.neighbour(*n) for n in NEIGHBOURS]
    peers += [place.partner()]
    peers += [device for _, _, device in place.plane()]
    peers += [device for _, _, device in place.ring()]
    for device in peers:
        pl.semaphore_signal(barrier, inc=1, device_id=device, device_id_type=MESH)
    return len(peers)


def remote(src, dst, send, recv, device):
    copy = pltpu.make_async_remote_copy(
        src_ref=src, dst_ref=dst, send_sem=send, recv_sem=recv, device_id=device, device_id_type=MESH
    )
    copy.start()
    return copy


class Halo:
    def __init__(self, k, place, s):
        self.k, self.place, self.s = k, place, s
        self.rows, self.width, _ = s["act_one"].shape
        self.pitch = self.width + 16
        self.copies = {}

    def line(self, r):
        start = (r + 1) * self.pitch + 8
        return pl.ds(start if isinstance(r, int) else pl.multiple_of(start, 8), self.width)

    def column(self, c):
        return pl.ds(self.pitch + 8 + c, self.rows, stride=self.pitch)

    def go(self, i, src, dst):
        k, s = self.k, self.s
        self.copies[i] = remote(
            src, dst, s["halo_send"].at[k, i], s["halo_recv"].at[k, i], self.place.neighbour(*NEIGHBOURS[i])
        )

    def send_rows(self, top, bottom):
        self.go(0, top, self.s["row_in"].at[self.k, 1])
        self.go(1, bottom, self.s["row_in"].at[self.k, 0])

    def send_columns(self, which, use):
        k, s, frame = self.k, self.s, self.s["frame"]
        s["col_out"][k, which, 0] = frame[self.column(0), :]
        s["col_out"][k, which, 1] = frame[self.column(self.width - 1), :]
        for i in use:
            down, right = NEIGHBOURS[i]
            src = s["col_out"].at[k, which, 0 if right < 0 else 1]
            self.go(i, src, s["col_in"].at[k, 1 if right < 0 else 0, 1 - down])

    def send_sides(self):
        self.send_columns(0, (2, 3))

    def send_corners(self):
        self.send_columns(1, (4, 5, 6, 7))

    def receive_sides(self):
        k, place, s, frame = self.k, self.place, self.s, self.s["frame"]
        for i in (2, 3):
            self.copies[i].wait()
        for side, there, c in ((0, place.lon > 0, -1), (1, place.lon < place.lon_size - 1, self.width)):
            frame[self.column(c), :] = jnp.where(there, s["col_in"][k, side, 1], 0.0)

    def receive_rest(self):
        k, place, s, frame = self.k, self.place, self.s, self.s["frame"]
        for i in (0, 1, 4, 5, 6, 7):
            self.copies[i].wait()
        rows, width, pitch = self.rows, self.width, self.pitch
        up = place.row_block > 0
        down = place.row_block < place.row_blocks - 1
        frame[self.line(-1), :] = jnp.where(up, s["row_in"][k, 0].astype(F32), 0.0)
        frame[self.line(rows), :] = jnp.where(down, s["row_in"][k, 1].astype(F32), 0.0)
        for side, there, c in ((0, place.lon > 0, -1), (1, place.lon < place.lon_size - 1, width)):
            got = s["col_in"]
            frame[pl.ds(8 + c, 1), :] = jnp.where(
                there & up, got[k, side, 0, pl.ds(rows - 1, 1), :], 0.0
            )
            frame[pl.ds((rows + 1) * pitch + 8 + c, 1), :] = jnp.where(
                there & down, got[k, side, 2, pl.ds(0, 1), :], 0.0
            )


def fill_patches(frame, patches, first, count, step, width):
    pitch = width + 16

    def body(i, carry):
        r = first + i * step
        to = pl.multiple_of(r * width, width)
        for b in range(3):
            window = frame[pl.ds(r * pitch + 7 + b, width), :]
            patches[pl.ds(to, width), b * 128 : (b + 1) * 128] = window.astype(BF)
        return carry

    lax.fori_loop(0, count, body, 0)


def fix_patches(frame, patches, rows, width):
    pitch = width + 16
    for r in range(1, rows + 1):
        patches[pl.ds(r * width, 16), :128] = frame[pl.ds(r * pitch + 7, 16), :].astype(BF)
        patches[pl.ds((r + 1) * width - 16, 16), 256:] = frame[
            pl.ds(r * pitch + width - 7, 16), :
        ].astype(BF)


def fill_weights(out, taps, channels):
    wide = 3 * channels
    out[pl.ds(3 * wide, wide), :channels] = jnp.zeros((wide, channels), BF)
    out[pl.ds(0, wide), channels:] = jnp.zeros((wide, channels), BF)
    for a in range(3):
        for b in range(3):
            tap = taps(a, b)
            for second in range(2):
                at = (a + second) * wide + b * channels
                out[at : at + channels, second * channels : (second + 1) * channels] = tap


def convolve(patches, weights, first, pairs, step, width, finish):
    def body(p, carry):
        r = first + p * step
        lines = [patches[pl.ds(pl.multiple_of((r + a) * width, width), width), :] for a in range(4)]
        both = dot(jnp.concatenate(lines, axis=1), weights[...])
        half = both.shape[1] // 2
        finish(r, both[:, :half])
        finish(r + 1, both[:, half:])
        return carry

    lax.fori_loop(0, pairs, body, 0)


def convolve_outer(patches, weights, rows, width, finish):
    wide, half = patches.shape[1], weights.shape[1] // 2

    def body(p, carry):
        r = p * (rows - 1)
        lines = [patches[pl.ds(pl.multiple_of((r + a) * width, width), width), :] for a in range(3)]
        finish(r, dot(jnp.concatenate(lines, axis=1), weights[: 3 * wide, :half]))
        return carry

    lax.fori_loop(0, 2, body, 0)


def kernel_grad(patches, upstream, acc, rows, width):
    channels = upstream.shape[2]
    upstream[0] = jnp.zeros((width, channels), BF)
    upstream[rows + 1] = jnp.zeros((width, channels), BF)
    group = rows // 2
    for g in range(2):
        left = patches[pl.ds((1 + g * group) * width, group * width), :]
        right = jnp.concatenate(
            [
                jnp.concatenate([upstream[1 + g * group + r + 1 - a] for a in range(3)], axis=1)
                for r in range(group)
            ],
            axis=0,
        )
        value = dot(left, right, ((0,), (0,)))
        if g == 0:
            acc[...] = value
        else:
            acc[...] += value
    acc[:, :channels] += dot(patches[pl.ds(0, width), :], upstream[1], ((0,), (0,)))
    acc[:, 2 * channels :] += dot(
        patches[pl.ds((rows + 1) * width, width), :], upstream[rows], ((0,), (0,))
    )


def joined(tile):
    total = jnp.sum(tile, axis=0, keepdims=True)
    high = total.astype(BF).astype(F32)
    row = lax.broadcasted_iota(jnp.int32, tile.shape, 0)
    return jnp.where(row == 0, high, jnp.where(row == 1, total - high, 0.0))


class Reduce:
    def __init__(self, name, place, s, spread, extra=False):
        self.place, self.spread, self.extra = place, spread, extra
        for part in ("part", "core", "half", "plane", "sum", "ring", "out", "send", "recv"):
            setattr(self, part, s[name + "_" + part])
        self.sems = 0

    def go(self, src, dst, i, device):
        return remote(src, dst, self.send.at[i], self.recv.at[i], device)

    def rounded(self, value):
        if not self.extra:
            return value.astype(BF)
        last = jnp.where(self.place.core == 1, joined(value[4]), value[4])
        return jnp.concatenate([value[:4], last[None]], axis=0).astype(BF)

    def step0(self):
        p = self.place
        self.copies = [self.go(self.part.at[1 - p.core], self.core, 0, p.partner())]

    def step1(self):
        p = self.place
        for copy in self.copies:
            copy.wait()

        def body(i, carry):
            value = self.part[p.core, i].astype(F32) + self.core[i].astype(F32)
            self.half[i] = self.rounded(value)
            return carry

        lax.fori_loop(0, p.nq, body, 0)
        self.copies = [
            self.go(self.half.at[q], self.plane.at[d], 1 + d, device) for d, q, device in p.plane()
        ]

    def step2(self):
        p = self.place
        for copy in self.copies:
            copy.wait()
        value = self.half[p.q].astype(F32)
        for d in range(1, p.nq):
            value = value + self.plane[d].astype(F32)
        self.sum[...] = self.rounded(value)
        if self.spread:
            self.ring[p.z] = self.sum[p.bin]
        else:
            self.ring[p.z] = self.sum[...]
        self.copies = [
            self.go(self.sum.at[zhi] if self.spread else self.sum, self.ring.at[p.z], 1 + p.nq + dz, device)
            for dz, zhi, device in p.ring()
        ]

    def step3(self):
        p = self.place
        for copy in self.copies:
            copy.wait()
        value = self.ring[0].astype(F32)
        for z in range(1, p.nz):
            value = value + self.ring[z].astype(F32)
        self.out[p.core, p.q] = self.rounded(value)
        mine = self.out.at[p.core, p.q]
        base = 1 + p.nq + p.nz
        self.copies = [self.go(mine, mine, base + d, device) for d, _, device in p.plane()]

    def step4(self):
        p = self.place
        for copy in self.copies:
            copy.wait()
        mine = self.out.at[p.core]
        self.copies = [self.go(mine, mine, 1 + 2 * p.nq + p.nz, p.partner())]

    def step5(self):
        for copy in self.copies:
            copy.wait()


def pack_grad(acc, part, channels):
    qr = part.shape[-2]
    for a in range(3):
        for b in range(3):
            c, t = divmod(3 * a + b, 5)
            tap = acc[b * channels : (b + 1) * channels, a * channels : (a + 1) * channels]
            part[c, :, t] = tap.reshape(channels // qr, qr, channels).astype(BF)


def unpack_grad(out, result, channels):
    for a in range(3):
        for b in range(3):
            c, t = divmod(3 * a + b, 5)
            result[a, b] = out[c, :, t].astype(F32).reshape(channels, channels)


def turned(tile):
    return jnp.transpose(tile.astype(F32)).astype(BF)


def load(src, dst, sem):
    copy = pltpu.make_async_copy(src, dst, sem)
    copy.start()
    return copy


def kernel(sizes, names, x_ref, w1_ref, w2_ref, hw_ref, tg_ref, g1_ref, g2_ref, gh_ref, *refs):
    lat, lon, bins, cells_all = sizes
    s = dict(zip(names, refs))
    place = Place(lat, lon, bins)
    rows, width, channels = x_ref.shape
    heads, total, _ = s["hw_rows"].shape
    bin_width = total // bins
    half_heads = heads // 2
    frame, hw_all = s["frame"], s["hw_all"]
    scale = 1.0 / math.sqrt(heads * cells_all)

    peers = enter(place)
    loads = [
        load(x_ref, s["x"], s["load"].at[0]),
        load(w1_ref, s["w1"], s["load"].at[1]),
        load(w2_ref, s["w2"], s["load"].at[2]),
        load(hw_ref, hw_all.at[place.bin], s["load"].at[3]),
        load(tg_ref.at[:, pl.ds(place.bin * rows, rows), :], s["tg"], s["load"].at[4]),
    ]
    pl.semaphore_wait(pltpu.get_barrier_semaphore(), peers)

    halo = Halo(0, place, s)
    my_heads = pl.ds(place.core * half_heads, half_heads)
    hw_copies = [
        remote(
            hw_ref.at[my_heads],
            hw_all.at[place.bin, my_heads],
            s["hw_send"].at[0, db],
            s["hw_recv"].at[0, db],
            device,
        )
        for db, device in place.bins()
    ]
    halo.send_rows(x_ref.at[0], x_ref.at[rows - 1])
    loads[0].wait()
    for r in range(rows):
        frame[halo.line(r), :] = s["x"][r].astype(F32)
    halo.send_sides()
    halo.send_corners()

    fill_patches(frame, s["px"], 1, rows, 1, width)
    loads[1].wait()
    fill_weights(s["w_one"], lambda a, b: s["w1"][a, b], channels)
    halo.receive_sides()
    fix_patches(frame, s["px"], rows, width)

    def finish_one(r, value):
        s["pre_one"][r] = value
        act = jnp.maximum(value, 0.0).astype(BF)
        s["act_one"][r] = act
        frame[halo.line(r), :] = act.astype(F32)

    convolve(s["px"], s["w_one"], 1, (rows - 2) // 2, 2, width, finish_one)
    halo.receive_rest()
    fill_patches(frame, s["px"], 0, 2, rows + 1, width)
    convolve_outer(s["px"], s["w_one"], rows, width, finish_one)
    halo = Halo(1, place, s)
    halo.send_sides()
    halo.send_rows(s["act_one"].at[0], s["act_one"].at[rows - 1])
    halo.send_corners()

    fill_patches(frame, s["pa"], 1, rows, 1, width)
    loads[2].wait()
    fill_weights(s["w_two"], lambda a, b: s["w2"][a, b], channels)
    for copy in hw_copies:
        copy.wait()
    hw_copies = []
    for db in range(1, bins):
        there = hw_all.at[(place.bin + db) % bins, my_heads]
        hw_copies.append(
            remote(there, there, s["hw_send"].at[1, db], s["hw_recv"].at[1, db], place.partner())
        )
    halo.receive_sides()
    fix_patches(frame, s["pa"], rows, width)

    def finish_two(r, value):
        s["pre_two"][r] = value
        s["act_two"][r] = jnp.maximum(value, 0.0).astype(BF)

    convolve(s["pa"], s["w_two"], 2, (rows - 4) // 2, 2, width, finish_two)

    for copy in loads[3:] + hw_copies:
        copy.wait()
    hw_rows, hw_cols = s["hw_rows"], s["hw_cols"]
    for b in range(bins):
        for k in range(heads):
            tile = hw_all[b, k]
            hw_cols[k, :, b * bin_width : (b + 1) * bin_width] = tile
            hw_rows[k, b * bin_width : (b + 1) * bin_width, :] = turned(tile)
    s["loss_acc"][...] = jnp.zeros_like(s["loss_acc"])
    last_halo = Halo(2, place, s)

    def heads_body(i, carry):
        r = (i + 2) % rows

        feat_t = turned(s["act_two"][r])
        back = jnp.zeros((channels, width), F32)
        loss = s["loss_acc"][...]
        eight = lax.broadcasted_iota(jnp.int32, (8, width), 0)
        group = lax.broadcasted_iota(jnp.int32, (total // 8, 8, width), 0)
        for k in range(heads):
            logits = dot(hw_rows[k], feat_t).reshape(total // 8, 8, width)
            highest = jnp.max(jnp.max(logits, axis=0), axis=0, keepdims=True)
            raised = jnp.exp(logits - highest[None])
            summed = jnp.sum(jnp.sum(raised, axis=0), axis=0, keepdims=True)
            label = s["tg"][k, pl.ds(r, 1), :] - eight
            chosen = group * 8 == label[None]
            picked = jnp.sum(jnp.sum(jnp.where(chosen, logits, 0.0), axis=0), axis=0, keepdims=True)
            loss = loss + (highest + jnp.log(summed) - picked)
            value = raised * (scale / summed)[None]
            grad = jnp.where(chosen, value - scale, value).reshape(total, width).astype(BF)
            s["head_grad"][r, k] = grad
            back = back + dot(hw_cols[k], grad)
        s["loss_acc"][...] = loss
        hidden = jnp.where(s["pre_two"][r] > 0, jnp.transpose(back), 0.0).astype(BF)
        s["back_two"][r + 1] = hidden
        frame[halo.line(r), :] = hidden.astype(F32)
        return carry

    lax.fori_loop(0, rows - 4, heads_body, 0)
    halo.receive_rest()
    fill_patches(frame, s["pa"], 0, 2, rows + 1, width)
    convolve(s["pa"], s["w_two"], 0, 2, rows - 2, width, finish_two)
    lax.fori_loop(rows - 4, rows - 1, heads_body, 0)
    last_halo.send_rows(s["back_two"].at[1], s["back_two"].at[rows])
    last_halo.send_corners()
    lax.fori_loop(rows - 1, rows, heads_body, 0)
    last_halo.send_sides()
    halo = last_halo

    gh = Reduce("gh", place, s, True)
    g2 = Reduce("g2", place, s, False, extra=True)
    g1 = Reduce("g1", place, s, False)
    qr = gh.part.shape[-2]
    feats = s["act_two"][...].reshape(rows * width, channels)
    for k in range(heads):
        c, kk = divmod(k, half_heads)
        grads = jnp.concatenate([s["head_grad"][r, k] for r in range(rows)], axis=1)
        value = dot(grads, feats).reshape(bins, bin_width // qr, qr, channels)
        for b in range(bins):
            gh.part[c, :, b, kk] = value[b].astype(BF)
    gh.step0()

    kernel_grad(s["pa"], s["back_two"], s["g_acc"], rows, width)
    pack_grad(s["g_acc"], g2.part, channels)
    loss = s["loss_acc"][...]
    lanes = loss[:, :128]
    for i in range(1, width // 128):
        lanes = lanes + loss[:, i * 128 : (i + 1) * 128]
    row = lax.broadcasted_iota(jnp.int32, (qr, 128), 0)
    loss_tile = joined(jnp.where(row == 0, lanes, 0.0)).astype(BF)
    for q in range(place.nq):
        g2.part[1, q, 4] = loss_tile
        g1.part[1, q, 4] = jnp.zeros((qr, channels), BF)
    g2.step0()

    fill_weights(s["w_flip"], lambda a, b: turned(s["w2"][2 - a, 2 - b]), channels)
    fill_patches(frame, s["pg"], 1, rows, 1, width)
    gh.step1()
    halo.receive_sides()
    fix_patches(frame, s["pg"], rows, width)
    halo.receive_rest()
    fill_patches(frame, s["pg"], 0, 2, rows + 1, width)

    def finish_back(r, value):
        s["back_one"][r + 1] = jnp.where(s["pre_one"][r] > 0, value, 0.0).astype(BF)

    convolve(s["pg"], s["w_flip"], 0, rows // 2, 2, width, finish_back)
    g2.step1()
    kernel_grad(s["px"], s["back_one"], s["g_acc"], rows, width)
    pack_grad(s["g_acc"], g1.part, channels)
    g1.step0()
    gh.step2()
    g1.step1()
    g2.step2()
    gh.step3()
    g1.step2()
    g2.step3()
    g1.step3()
    gh.step4()
    g2.step4()
    gh.step5()
    stores = [load(gh.out, gh_ref, s["store"].at[0])]
    g2.step5()
    stores.append(load(g2.out, g2_ref, s["store"].at[1]))
    g1.step4()
    stores.append(load(g1.out.at[place.core], g1_ref.at[place.core], s["store"].at[2]))
    g1.step5()
    other = 1 - place.core
    stores.append(load(g1.out.at[other], g1_ref.at[other], s["store"].at[3]))
    for copy in stores:
        copy.wait()


def unpack(count, g1_in, g2_in, gh_in, loss_ref, g1_ref, g2_ref, gh_ref):
    heads, channels, bin_width = gh_ref.shape
    for k in range(heads):
        c, kk = divmod(k, heads // 2)
        gh_ref[k] = jnp.transpose(gh_in[c, :, kk].astype(F32).reshape(bin_width, channels))
    unpack_grad(g2_in, g2_ref, channels)
    unpack_grad(g1_in, g1_ref, channels)
    whole = jnp.sum(g2_in[1, 0, 4].astype(F32), axis=0, keepdims=True)
    loss_ref[...] = jnp.sum(whole, axis=1, keepdims=True) * (1.0 / count)


def per_device(inputs, conv_one, conv_two, head_weight, targets):
    rows, width, channels = inputs.shape
    heads, _, bin_width = head_weight.shape
    lat, lon, bins = (lax.axis_size(a) for a in ("lat", "lon", "bin"))
    cells_all = rows * lat * bins * width * lon
    scratch = plan(lat, lon, bins, rows, width, channels, heads, bin_width)
    vmem = pl.BlockSpec(memory_space=pltpu.VMEM)
    hbm = pl.BlockSpec(memory_space=pl.ANY)
    parts = pl.pallas_call(
        functools.partial(kernel, (lat, lon, bins, cells_all), tuple(scratch)),
        out_shape=[
            jax.ShapeDtypeStruct(scratch[name + "_out"].shape, BF) for name in ("g1", "g2", "gh")
        ],
        in_specs=[hbm] * 5,
        out_specs=[hbm] * 3,
        scratch_shapes=list(scratch.values()),
        compiler_params=pltpu.CompilerParams(
            collective_id=0, has_side_effects=True, vmem_limit_bytes=60 << 20
        ),
    )(inputs, conv_one, conv_two, head_weight, targets)
    loss, g1, g2, gh = pl.pallas_call(
        functools.partial(unpack, heads * cells_all),
        out_shape=[
            jax.ShapeDtypeStruct((1, 1), F32),
            jax.ShapeDtypeStruct(conv_one.shape, F32),
            jax.ShapeDtypeStruct(conv_two.shape, F32),
            jax.ShapeDtypeStruct(head_weight.shape, F32),
        ],
        in_specs=[vmem] * 3,
        out_specs=[vmem] * 4,
    )(*parts)
    return (loss.reshape(()), g1, g2, gh)


def solution(mesh):
    in_specs = (
        P(("lat", "bin"), "lon", None),
        P(),
        P(),
        P(None, None, "bin"),
        P(None, "lat", "lon"),
    )
    out_specs = (P(), P(), P(), P(None, None, "bin"))
    return jax.shard_map(
        per_device, mesh=mesh, in_specs=in_specs, out_specs=out_specs, check_vma=False
    )
```

```python
import functools
import math

import jax
import jax.numpy as jnp
from jax import lax
from jax.experimental import pallas as pl
from jax.experimental.pallas import tpu as pltpu
from jax.sharding import PartitionSpec as P

BF = jnp.bfloat16
F32 = jnp.float32
MESH = pl.DeviceIdType.MESH
CORES = 2
PLANE_X = 4


def dot(left, right, contract=((1,), (0,))):
    return lax.dot_general(left, right, (contract, ((), ())), preferred_element_type=F32)


def layout(lat, lon, bins):
    plane_x = min(PLANE_X, lat // CORES)
    return dict(nx=plane_x, nzl=lat // (CORES * plane_x), ny=lon, nzh=bins)


def plan(lat, lon, bins, rows, width, channels, heads, bin_width):
    d = layout(lat, lon, bins)
    nq, nz = d["nx"] * d["ny"], d["nzl"] * d["nzh"]
    qr = channels // nq
    pitch = width + 16
    total = bins * bin_width
    vm, dma = pltpu.VMEM, pltpu.SemaphoreType.DMA
    s = dict(
        frame=vm(((rows + 2) * pitch, channels), F32),
        px=vm(((rows + 2) * width, 3 * channels), BF),
        pa=vm(((rows + 2) * width, 3 * channels), BF),
        pg=vm(((rows + 2) * width, 3 * channels), BF),
        w_one=vm((12 * channels, 2 * channels), BF),
        w_two=vm((12 * channels, 2 * channels), BF),
        w_flip=vm((12 * channels, 2 * channels), BF),
        act_one=vm((rows, width, channels), BF),
        act_two=vm((rows, width, channels), BF),
        back_two=vm((rows + 2, width, channels), BF),
        back_one=vm((rows + 2, width, channels), BF),
        pre_one=vm((rows, width, channels), F32),
        pre_two=vm((rows, width, channels), F32),
        hw_all=vm((bins, heads, channels, bin_width), BF),
        hw_rows=vm((heads, total, channels), BF),
        hw_cols=vm((heads, channels, total), BF),
        head_grad=vm((rows, heads, total, width), BF),
        x=vm((rows, width, channels), BF),
        w1=vm((3, 3, channels, channels), BF),
        w2=vm((3, 3, channels, channels), BF),
        tg=vm((heads, rows, width), jnp.int32),
        load=dma((5,)),
        store=dma((6,)),
        loss_acc=vm((1, width), F32),
        act_turned=vm((rows, channels, width), BF),
        back_acc=vm((rows, channels, width), F32),
        g_acc=vm((3 * channels, 3 * channels), F32),
        col_out=vm((3, 3, 2, rows, channels), F32),
        col_in=vm((3, 2, 4, rows, channels), F32),
        row_in=vm((3, 2, width, channels), BF),
        halo_send=dma((3, 10)),
        halo_recv=dma((3, 10)),
        hw_send=dma((2, 2, bins)),
        hw_recv=dma((2, 2, bins)),
    )
    for name, (first, second) in dict(early=(2 * bins + 5, 7), late=(5, 5)).items():
        tile = (qr, channels)
        s[name + "_part"] = vm((2, nq, first) + tile, BF)
        s[name + "_core"] = vm((nq, first) + tile, BF)
        s[name + "_half"] = vm((nq, first) + tile, BF)
        s[name + "_plane"] = vm((nq, first) + tile, BF)
        s[name + "_sum"] = vm((bins, second) + tile, BF)
        s[name + "_ring"] = vm((nz, second) + tile, BF)
        s[name + "_out"] = vm((2, nq, second) + tile, BF)
        s[name + "_send"] = dma((2 + 2 * nq + nz,))
        s[name + "_recv"] = dma((2 + 2 * nq + nz,))
    return s


class Place:
    def __init__(self, lat, lon, bins):
        self.__dict__.update(layout(lat, lon, bins))
        self.lat_size, self.lon_size, self.bin_size = lat, lon, bins
        self.lat, self.lon, self.bin = (lax.axis_index(a) for a in ("lat", "lon", "bin"))
        self.core = self.lat % CORES
        self.x = (self.lat // CORES) % self.nx
        self.zlo = self.lat // (CORES * self.nx)
        self.y = self.lon
        self.nq, self.nz = self.nx * self.ny, self.nzl * self.nzh
        self.z = self.bin * self.nzl + self.zlo
        self.q = self.x * self.ny + self.y
        self.row_block = self.lat * bins + self.bin
        self.row_blocks = lat * bins

    def device(self, lat=None, lon=None, bin=None):
        pick = lambda v, own: own if v is None else v
        return dict(lat=pick(lat, self.lat), lon=pick(lon, self.lon), bin=pick(bin, self.bin))

    def at(self, core=None, x=None, zlo=None):
        core = self.core if core is None else core
        x = self.x if x is None else x
        zlo = self.zlo if zlo is None else zlo
        return (zlo * self.nx + x) * CORES + core

    def partner(self):
        return self.device(lat=self.at(core=1 - self.core))

    def plane(self):
        for dx in range(self.nx):
            for dy in range(self.ny):
                if dx or dy:
                    x, y = (self.x + dx) % self.nx, (self.y + dy) % self.ny
                    yield dx * self.ny + dy, x * self.ny + y, self.device(lat=self.at(x=x), lon=y)

    def ring(self):
        for dz in range(1, self.nz):
            z = (self.z + dz) % self.nz
            zhi, zlo = z // self.nzl, z % self.nzl
            yield dz, zhi, self.device(lat=self.at(zlo=zlo), bin=zhi)

    def bins(self):
        if self.nzl == 2 and self.bin_size == 4:
            side = 2 * self.zlo - 1
            for step, other in ((1, True), (2, True), (1, False)):
                zlo = 1 - self.zlo if other else self.zlo
                to = (self.bin + step * side + 4) % 4
                source = (self.bin + (step if other else -step) * side + 4) % 4
                yield source, self.device(lat=self.at(zlo=zlo), bin=to)
        else:
            for step in range(1, self.bin_size):
                to = (self.bin + step) % self.bin_size
                yield (self.bin - step + self.bin_size) % self.bin_size, self.device(bin=to)

    def neighbour(self, down, right):
        block = (self.row_block + down) % self.row_blocks
        return self.device(
            lat=block // self.bin_size, lon=(self.lon + right) % self.lon_size, bin=block % self.bin_size
        )


NEIGHBOURS = [(-1, 0), (1, 0), (0, -1), (0, 1), (-1, -1), (-1, 1), (1, -1), (1, 1)]
EARLY = (8, 9)


def enter(place):
    barrier = pltpu.get_barrier_semaphore()
    peers = [place.neighbour(*n) for n in NEIGHBOURS]
    peers += [place.partner()]
    peers += [device for _, _, device in place.plane()]
    peers += [device for _, _, device in place.ring()]
    for device in peers:
        pl.semaphore_signal(barrier, inc=1, device_id=device, device_id_type=MESH)
    return len(peers)


def remote(src, dst, send, recv, device):
    copy = pltpu.make_async_remote_copy(
        src_ref=src, dst_ref=dst, send_sem=send, recv_sem=recv, device_id=device, device_id_type=MESH
    )
    copy.start()
    return copy


class Halo:
    def __init__(self, k, place, s):
        self.k, self.place, self.s = k, place, s
        self.rows, self.width, _ = s["act_one"].shape
        self.pitch = self.width + 16
        self.copies = {}

    def line(self, r):
        start = (r + 1) * self.pitch + 8
        return pl.ds(start if isinstance(r, int) else pl.multiple_of(start, 8), self.width)

    def column(self, c):
        return pl.ds(self.pitch + 8 + c, self.rows, stride=self.pitch)

    def go(self, i, src, dst):
        k, s = self.k, self.s
        self.copies[i] = remote(
            src, dst, s["halo_send"].at[k, i], s["halo_recv"].at[k, i], self.place.neighbour(*NEIGHBOURS[i - 6 if i in EARLY else i])
        )

    def send_rows(self, top, bottom):
        self.go(0, top, self.s["row_in"].at[self.k, 1])
        self.go(1, bottom, self.s["row_in"].at[self.k, 0])

    def send_columns(self, which, use):
        k, s, frame = self.k, self.s, self.s["frame"]
        s["col_out"][k, which, 0] = frame[self.column(0), :]
        s["col_out"][k, which, 1] = frame[self.column(self.width - 1), :]
        for i in use:
            down, right = NEIGHBOURS[i - 6 if i in EARLY else i]
            src = s["col_out"].at[k, which, 0 if right < 0 else 1]
            self.go(i, src, s["col_in"].at[k, 1 if right < 0 else 0, 3 if i in EARLY else 1 - down])

    def send_sides(self):
        self.send_columns(0, (2, 3))

    def send_early_sides(self):
        self.send_columns(2, EARLY)

    def send_corners(self):
        self.send_columns(1, (4, 5, 6, 7))

    def receive_sides(self, early=False):
        k, place, s, frame = self.k, self.place, self.s, self.s["frame"]
        for i in EARLY if early else (2, 3):
            self.copies[i].wait()
        for side, there, c in ((0, place.lon > 0, -1), (1, place.lon < place.lon_size - 1, self.width)):
            frame[self.column(c), :] = jnp.where(there, s["col_in"][k, side, 3 if early else 1], 0.0)

    def receive_rest(self):
        k, place, s, frame = self.k, self.place, self.s, self.s["frame"]
        for i in (0, 1, 4, 5, 6, 7):
            self.copies[i].wait()
        rows, width, pitch = self.rows, self.width, self.pitch
        up = place.row_block > 0
        down = place.row_block < place.row_blocks - 1
        frame[self.line(-1), :] = jnp.where(up, s["row_in"][k, 0].astype(F32), 0.0)
        frame[self.line(rows), :] = jnp.where(down, s["row_in"][k, 1].astype(F32), 0.0)
        for side, there, c in ((0, place.lon > 0, -1), (1, place.lon < place.lon_size - 1, width)):
            got = s["col_in"]
            frame[pl.ds(8 + c, 1), :] = jnp.where(
                there & up, got[k, side, 0, pl.ds(rows - 1, 1), :], 0.0
            )
            frame[pl.ds((rows + 1) * pitch + 8 + c, 1), :] = jnp.where(
                there & down, got[k, side, 2, pl.ds(0, 1), :], 0.0
            )


def fill_patches(frame, patches, first, count, step, width):
    pitch = width + 16

    def body(i, carry):
        r = first + i * step
        to = pl.multiple_of(r * width, width)
        for b in range(3):
            window = frame[pl.ds(r * pitch + 7 + b, width), :]
            patches[pl.ds(to, width), b * 128 : (b + 1) * 128] = window.astype(BF)
        return carry

    lax.fori_loop(0, count, body, 0)


def fix_patches(frame, patches, lines, width):
    pitch = width + 16
    for r in lines:
        patches[pl.ds(r * width, 16), :128] = frame[pl.ds(r * pitch + 7, 16), :].astype(BF)
        patches[pl.ds((r + 1) * width - 16, 16), 256:] = frame[
            pl.ds(r * pitch + width - 7, 16), :
        ].astype(BF)


def fill_weights(out, taps, channels):
    wide = 3 * channels
    out[pl.ds(3 * wide, wide), :channels] = jnp.zeros((wide, channels), BF)
    out[pl.ds(0, wide), channels:] = jnp.zeros((wide, channels), BF)
    for a in range(3):
        for b in range(3):
            tap = taps(a, b)
            for second in range(2):
                at = (a + second) * wide + b * channels
                out[at : at + channels, second * channels : (second + 1) * channels] = tap


def convolve(patches, weights, first, pairs, step, width, finish):
    def body(p, carry):
        r = first + p * step
        lines = [patches[pl.ds(pl.multiple_of((r + a) * width, width), width), :] for a in range(4)]
        both = dot(jnp.concatenate(lines, axis=1), weights[...])
        half = both.shape[1] // 2
        finish(r, both[:, :half])
        finish(r + 1, both[:, half:])
        return carry

    lax.fori_loop(0, pairs, body, 0)


def convolve_outer(patches, weights, rows, width, finish):
    wide, half = patches.shape[1], weights.shape[1] // 2

    def body(p, carry):
        r = p * (rows - 1)
        lines = [patches[pl.ds(pl.multiple_of((r + a) * width, width), width), :] for a in range(3)]
        finish(r, dot(jnp.concatenate(lines, axis=1), weights[: 3 * wide, :half]))
        return carry

    lax.fori_loop(0, 2, body, 0)


def kernel_grad(patches, upstream, acc, rows, width):
    channels = upstream.shape[2]
    upstream[0] = jnp.zeros((width, channels), BF)
    upstream[rows + 1] = jnp.zeros((width, channels), BF)
    group = rows // 2
    for g in range(2):
        left = patches[pl.ds((1 + g * group) * width, group * width), :]
        right = jnp.concatenate(
            [
                jnp.concatenate([upstream[1 + g * group + r + 1 - a] for a in range(3)], axis=1)
                for r in range(group)
            ],
            axis=0,
        )
        value = dot(left, right, ((0,), (0,)))
        if g == 0:
            acc[...] = value
        else:
            acc[...] += value
    acc[:, :channels] += dot(patches[pl.ds(0, width), :], upstream[1], ((0,), (0,)))
    acc[:, 2 * channels :] += dot(
        patches[pl.ds((rows + 1) * width, width), :], upstream[rows], ((0,), (0,))
    )


def joined(tile):
    total = jnp.sum(tile, axis=0, keepdims=True)
    high = total.astype(BF).astype(F32)
    row = lax.broadcasted_iota(jnp.int32, tile.shape, 0)
    return jnp.where(row == 0, high, jnp.where(row == 1, total - high, 0.0))


class Reduce:
    def __init__(self, name, place, s, heads=0):
        self.place, self.heads = place, heads
        for part in ("part", "core", "half", "plane", "sum", "ring", "out", "send", "recv"):
            setattr(self, part, s[name + "_" + part])
        self.sems = 0

    def go(self, src, dst, i, device):
        return remote(src, dst, self.send.at[i], self.recv.at[i], device)

    def rounded(self, value):
        if not self.heads:
            return value.astype(BF)
        last = jnp.where(self.place.core == 1, joined(value[-1]), value[-1])
        return jnp.concatenate([value[:-1], last[None]], axis=0).astype(BF)

    def step0(self):
        p = self.place
        self.copies = [self.go(self.part.at[1 - p.core], self.core, 0, p.partner())]

    def step1(self):
        p = self.place
        for copy in self.copies:
            copy.wait()

        def body(i, carry):
            value = self.part[p.core, i].astype(F32) + self.core[i].astype(F32)
            self.half[i] = self.rounded(value)
            return carry

        lax.fori_loop(0, p.nq, body, 0)
        self.copies = [
            self.go(self.half.at[q], self.plane.at[d], 1 + d, device) for d, q, device in p.plane()
        ]

    def step2(self):
        p = self.place
        for copy in self.copies:
            copy.wait()
        value = self.half[p.q].astype(F32)
        for d in range(1, p.nq):
            value = value + self.plane[d].astype(F32)
        value = self.rounded(value)
        if self.heads:
            for b in range(p.bin_size):
                own = value[2 * b : 2 * b + 2]
                self.sum[b] = jnp.concatenate([own, value[self.heads :]], axis=0)
        else:
            self.sum[0] = value
        mine = p.bin if self.heads else 0
        self.ring[p.z] = self.sum[mine]
        self.copies = [
            self.go(self.sum.at[zhi if self.heads else 0], self.ring.at[p.z], 1 + p.nq + dz, device)
            for dz, zhi, device in p.ring()
        ]

    def step3(self):
        p = self.place
        for copy in self.copies:
            copy.wait()
        value = self.ring[0].astype(F32)
        for z in range(1, p.nz):
            value = value + self.ring[z].astype(F32)
        self.out[p.core, p.q] = self.rounded(value)
        mine = self.out.at[p.core, p.q]
        base = 1 + p.nq + p.nz
        self.copies = [self.go(mine, mine, base + d, device) for d, _, device in p.plane()]

    def step4(self):
        p = self.place
        for copy in self.copies:
            copy.wait()
        mine = self.out.at[p.core]
        self.copies = [self.go(mine, mine, 1 + 2 * p.nq + p.nz, p.partner())]

    def step5(self):
        for copy in self.copies:
            copy.wait()


def pack_grad(acc, part, channels, first=0):
    qr = part.shape[-2]
    for a in range(3):
        for b in range(3):
            c, t = divmod(3 * a + b, 5)
            tap = acc[b * channels : (b + 1) * channels, a * channels : (a + 1) * channels]
            part[c, :, first + t] = tap.reshape(channels // qr, qr, channels).astype(BF)


def unpack_grad(out, result, channels, first=0):
    for a in range(3):
        for b in range(3):
            c, t = divmod(3 * a + b, 5)
            result[a, b] = out[c, :, first + t].astype(F32).reshape(channels, channels)


def turned(tile):
    return jnp.transpose(tile.astype(F32)).astype(BF)


def load(src, dst, sem):
    copy = pltpu.make_async_copy(src, dst, sem)
    copy.start()
    return copy


def kernel(sizes, names, x_ref, w1_ref, w2_ref, hw_ref, tg_ref, late_ref, early_ref, *refs):
    lat, lon, bins, cells_all = sizes
    s = dict(zip(names, refs))
    place = Place(lat, lon, bins)
    rows, width, channels = x_ref.shape
    heads, total, _ = s["hw_rows"].shape
    bin_width = total // bins
    half_heads = heads // 2
    frame, hw_all = s["frame"], s["hw_all"]
    scale = 1.0 / math.sqrt(heads * cells_all)

    peers = enter(place)
    loads = [
        load(x_ref, s["x"], s["load"].at[0]),
        load(w1_ref, s["w1"], s["load"].at[1]),
        load(w2_ref, s["w2"], s["load"].at[2]),
        load(hw_ref, hw_all.at[place.bin], s["load"].at[3]),
        load(tg_ref.at[:, pl.ds(place.bin * rows, rows), :], s["tg"], s["load"].at[4]),
    ]
    pl.semaphore_wait(pltpu.get_barrier_semaphore(), peers)

    halo = Halo(0, place, s)
    own_first = place.core * half_heads
    hw_copies = [[], []]
    sources = [source for source, _ in place.bins()]

    def send_head(kk):
        k = own_first + kk
        for j, (_, device) in enumerate(place.bins()):
            hw_copies[kk].append(
                remote(
                    hw_ref.at[k],
                    hw_all.at[place.bin, k],
                    s["hw_send"].at[0, kk, j],
                    s["hw_recv"].at[0, kk, j],
                    device,
                )
            )

    forwards = [[], []]

    def forward_head(kk):
        for j, source in enumerate(sources):
            hw_copies[kk][j].wait()
            there = hw_all.at[source, own_first + kk]
            forwards[kk].append(
                remote(
                    there, there, s["hw_send"].at[1, kk, j], s["hw_recv"].at[1, kk, j], place.partner()
                )
            )

    send_head(0)
    halo.send_rows(x_ref.at[0], x_ref.at[rows - 1])
    loads[0].wait()
    for r in range(rows):
        frame[halo.line(r), :] = s["x"][r].astype(F32)
    halo.send_sides()
    halo.send_corners()
    send_head(1)

    fill_patches(frame, s["px"], 1, rows, 1, width)
    loads[1].wait()
    fill_weights(s["w_one"], lambda a, b: s["w1"][a, b], channels)
    halo.receive_sides()
    fix_patches(frame, s["px"], range(1, rows + 1), width)

    def finish_one(r, value):
        s["pre_one"][r] = value
        act = jnp.maximum(value, 0.0).astype(BF)
        s["act_one"][r] = act
        frame[halo.line(r), :] = act.astype(F32)

    convolve(s["px"], s["w_one"], 1, (rows - 2) // 2, 2, width, finish_one)
    next_halo = Halo(1, place, s)
    next_halo.send_early_sides()
    halo.receive_rest()
    fill_patches(frame, s["px"], 0, 2, rows + 1, width)
    convolve_outer(s["px"], s["w_one"], rows, width, finish_one)
    halo = next_halo
    halo.send_sides()
    halo.send_rows(s["act_one"].at[0], s["act_one"].at[rows - 1])
    halo.send_corners()

    fill_patches(frame, s["pa"], 1, rows, 1, width)
    loads[2].wait()
    fill_weights(s["w_two"], lambda a, b: s["w2"][a, b], channels)
    fill_weights(s["w_flip"], lambda a, b: turned(s["w2"][2 - a, 2 - b]), channels)
    halo.receive_sides(early=True)
    fix_patches(frame, s["pa"], range(1, rows + 1), width)

    def finish_two(r, value):
        s["pre_two"][r] = value
        act = jnp.maximum(value, 0.0).astype(BF)
        s["act_two"][r] = act
        s["act_turned"][r] = turned(act)

    convolve(s["pa"], s["w_two"], 2, (rows - 4) // 2, 2, width, finish_two)

    for copy in loads[3:]:
        copy.wait()
    hw_rows, hw_cols, back_acc = s["hw_rows"], s["hw_cols"], s["back_acc"]
    s["loss_acc"][...] = jnp.zeros_like(s["loss_acc"])
    back_acc[...] = jnp.zeros_like(back_acc)
    last_halo = Halo(2, place, s)

    def prepare_head(k):
        for b in range(bins):
            tile = hw_all[b, k]
            hw_cols[k, :, b * bin_width : (b + 1) * bin_width] = tile
            hw_rows[k, b * bin_width : (b + 1) * bin_width, :] = turned(tile)

    def head_unit(k, pair):
        eight = lax.broadcasted_iota(jnp.int32, (8, width), 0)
        group = lax.broadcasted_iota(jnp.int32, (total // 8, 8, width), 0)
        loss = s["loss_acc"][...]
        logits = [dot(hw_rows[k], s["act_turned"][r]).reshape(total // 8, 8, width) for r in pair]
        for r, value in zip(pair, logits):
            highest = jnp.max(jnp.max(value, axis=0), axis=0, keepdims=True)
            raised = jnp.exp(value - highest[None])
            summed = jnp.sum(jnp.sum(raised, axis=0), axis=0, keepdims=True)
            label = s["tg"][k, pl.ds(r, 1), :] - eight
            chosen = group * 8 == label[None]
            picked = jnp.sum(jnp.sum(jnp.where(chosen, value, 0.0), axis=0), axis=0, keepdims=True)
            loss = loss + (highest + jnp.log(summed) - picked)
            prob = raised * (scale / summed)[None]
            grad = jnp.where(chosen, prob - scale, prob).reshape(total, width).astype(BF)
            s["head_grad"][r, k] = grad
            back_acc[r] += dot(hw_cols[k], grad)
        s["loss_acc"][...] = loss

    def head_row(r):
        eight = lax.broadcasted_iota(jnp.int32, (8, width), 0)
        group = lax.broadcasted_iota(jnp.int32, (total // 8, 8, width), 0)
        loss = s["loss_acc"][...]
        back = jnp.zeros((channels, width), F32)
        for k in range(heads):
            value = dot(hw_rows[k], s["act_turned"][r]).reshape(total // 8, 8, width)
            highest = jnp.max(jnp.max(value, axis=0), axis=0, keepdims=True)
            raised = jnp.exp(value - highest[None])
            summed = jnp.sum(jnp.sum(raised, axis=0), axis=0, keepdims=True)
            label = s["tg"][k, pl.ds(r, 1), :] - eight
            chosen = group * 8 == label[None]
            picked = jnp.sum(jnp.sum(jnp.where(chosen, value, 0.0), axis=0), axis=0, keepdims=True)
            loss = loss + (highest + jnp.log(summed) - picked)
            prob = raised * (scale / summed)[None]
            grad = jnp.where(chosen, prob - scale, prob).reshape(total, width).astype(BF)
            s["head_grad"][r, k] = grad
            back = back + dot(hw_cols[k], grad)
        s["loss_acc"][...] = loss
        back_acc[r] = back
        finish_heads(r)

    def finish_heads(r):
        hidden = jnp.where(s["pre_two"][r] > 0, jnp.transpose(back_acc[r]), 0.0).astype(BF)
        s["back_two"][r + 1] = hidden
        frame[halo.line(r), :] = hidden.astype(F32)

    def loop(count, body):
        lax.fori_loop(0, count, lambda i, carry: (body(i), carry)[1], 0)

    for kk in range(heads):
        k = (own_first + kk) % heads
        if kk < half_heads:
            forward_head(kk)
        else:
            for copy in forwards[kk - half_heads]:
                copy.wait()
        prepare_head(k)
        loop((rows - 4) // 2, lambda i: head_unit(k, (2 + 2 * i, 3 + 2 * i)))
    loop(rows - 4, lambda i: finish_heads(2 + i))
    halo.receive_sides()
    fix_patches(frame, s["pa"], (1, rows), width)
    halo.receive_rest()
    fill_patches(frame, s["pa"], 0, 2, rows + 1, width)
    convolve(s["pa"], s["w_two"], 0, 2, rows - 2, width, finish_two)
    loop(2, lambda i: head_row((rows - 1) * i))
    last_halo.send_rows(s["back_two"].at[1], s["back_two"].at[rows])
    last_halo.send_corners()
    loop(2, lambda i: head_row(1 + (rows - 3) * i))
    last_halo.send_sides()
    halo = last_halo

    early = Reduce("early", place, s, heads=2 * bins)
    late = Reduce("late", place, s)
    qr = early.part.shape[-2]
    feats = s["act_two"][...].reshape(rows * width, channels)
    for k in range(heads):
        c, kk = divmod(k, half_heads)
        grads = jnp.concatenate([s["head_grad"][r, k] for r in range(rows)], axis=1)
        value = dot(grads, feats).reshape(bins, bin_width // qr, qr, channels)
        for b in range(bins):
            early.part[c, :, 2 * b + kk] = value[b].astype(BF)
    kernel_grad(s["pa"], s["back_two"], s["g_acc"], rows, width)
    pack_grad(s["g_acc"], early.part, channels, 2 * bins)
    loss = s["loss_acc"][...]
    lanes = loss[:, :128]
    for i in range(1, width // 128):
        lanes = lanes + loss[:, i * 128 : (i + 1) * 128]
    row = lax.broadcasted_iota(jnp.int32, (qr, 128), 0)
    loss_tile = joined(jnp.where(row == 0, lanes, 0.0)).astype(BF)
    for q in range(place.nq):
        early.part[1, q, 2 * bins + 4] = loss_tile
        late.part[1, q, 4] = jnp.zeros((qr, channels), BF)
    early.step0()

    fill_patches(frame, s["pg"], 1, rows, 1, width)
    early.step1()
    halo.receive_sides()
    fix_patches(frame, s["pg"], range(1, rows + 1), width)
    halo.receive_rest()
    fill_patches(frame, s["pg"], 0, 2, rows + 1, width)

    def finish_back(r, value):
        s["back_one"][r + 1] = jnp.where(s["pre_one"][r] > 0, value, 0.0).astype(BF)

    convolve(s["pg"], s["w_flip"], 0, rows // 2, 2, width, finish_back)
    kernel_grad(s["px"], s["back_one"], s["g_acc"], rows, width)
    pack_grad(s["g_acc"], late.part, channels)
    late.step0()
    late.step1()
    early.step2()
    late.step2()
    early.step3()
    late.step3()
    early.step4()
    early.step5()
    stores = [load(early.out, early_ref, s["store"].at[0])]
    late.step4()
    stores.append(load(late.out.at[place.core], late_ref.at[place.core], s["store"].at[1]))
    late.step5()
    other = 1 - place.core
    stores.append(load(late.out.at[other], late_ref.at[other], s["store"].at[2]))
    for copy in stores:
        copy.wait()


def unpack(count, late_in, early_in, loss_ref, g1_ref, g2_ref, gh_ref):
    heads, channels, bin_width = gh_ref.shape
    for k in range(heads):
        c, kk = divmod(k, heads // 2)
        gh_ref[k] = jnp.transpose(early_in[c, :, kk].astype(F32).reshape(bin_width, channels))
    unpack_grad(early_in, g2_ref, channels, 2)
    unpack_grad(late_in, g1_ref, channels)
    whole = jnp.sum(early_in[1, 0, 6].astype(F32), axis=0, keepdims=True)
    loss_ref[...] = jnp.sum(whole, axis=1, keepdims=True) * (1.0 / count)


def per_device(inputs, conv_one, conv_two, head_weight, targets):
    rows, width, channels = inputs.shape
    heads, _, bin_width = head_weight.shape
    lat, lon, bins = (lax.axis_size(a) for a in ("lat", "lon", "bin"))
    cells_all = rows * lat * bins * width * lon
    scratch = plan(lat, lon, bins, rows, width, channels, heads, bin_width)
    vmem = pl.BlockSpec(memory_space=pltpu.VMEM)
    hbm = pl.BlockSpec(memory_space=pl.ANY)
    parts = pl.pallas_call(
        functools.partial(kernel, (lat, lon, bins, cells_all), tuple(scratch)),
        out_shape=[
            jax.ShapeDtypeStruct(scratch[name + "_out"].shape, BF) for name in ("late", "early")
        ],
        in_specs=[hbm] * 5,
        out_specs=[hbm] * 2,
        scratch_shapes=list(scratch.values()),
        compiler_params=pltpu.CompilerParams(
            collective_id=0, has_side_effects=True, vmem_limit_bytes=60 << 20
        ),
    )(inputs, conv_one, conv_two, head_weight, targets)
    loss, g1, g2, gh = pl.pallas_call(
        functools.partial(unpack, heads * cells_all),
        out_shape=[
            jax.ShapeDtypeStruct((1, 1), F32),
            jax.ShapeDtypeStruct(conv_one.shape, F32),
            jax.ShapeDtypeStruct(conv_two.shape, F32),
            jax.ShapeDtypeStruct(head_weight.shape, F32),
        ],
        in_specs=[vmem] * 2,
        out_specs=[vmem] * 4,
    )(*parts)
    return (loss.reshape(()), g1, g2, gh)


def solution(mesh):
    in_specs = (
        P(("lat", "bin"), "lon", None),
        P(),
        P(),
        P(None, None, "bin"),
        P(None, "lat", "lon"),
    )
    out_specs = (P(), P(), P(), P(None, None, "bin"))
    return jax.shard_map(
        per_device, mesh=mesh, in_specs=in_specs, out_specs=out_specs, check_vma=False
    )
```

```python
import functools
import math

import jax
import jax.numpy as jnp
from jax import lax
from jax.experimental import pallas as pl
from jax.experimental.pallas import tpu as pltpu
from jax.sharding import PartitionSpec as P

BF = jnp.bfloat16
F32 = jnp.float32
MESH = pl.DeviceIdType.MESH
CORES = 2
PLANE_X = 4


def dot(left, right, contract=((1,), (0,))):
    return lax.dot_general(left, right, (contract, ((), ())), preferred_element_type=F32)


def layout(lat, lon, bins):
    plane_x = min(PLANE_X, lat // CORES)
    return dict(nx=plane_x, nzl=lat // (CORES * plane_x), ny=lon, nzh=bins)


def plan(lat, lon, bins, rows, width, channels, heads, bin_width):
    d = layout(lat, lon, bins)
    nq, nz = d["nx"] * d["ny"], d["nzl"] * d["nzh"]
    qr = channels // nq
    pitch = width + 16
    total = bins * bin_width
    vm, dma = pltpu.VMEM, pltpu.SemaphoreType.DMA
    s = dict(
        frame=vm(((rows + 2) * pitch, channels), F32),
        px=vm(((rows + 2) * width, 3 * channels), BF),
        pa=vm(((rows + 2) * width, 3 * channels), BF),
        pg=vm(((rows + 2) * width, 3 * channels), BF),
        w_one=vm((12 * channels, 2 * channels), BF),
        w_two=vm((12 * channels, 2 * channels), BF),
        w_flip=vm((12 * channels, 2 * channels), BF),
        act_one=vm((rows, width, channels), BF),
        act_two=vm((rows, width, channels), BF),
        back_two=vm((rows + 2, width, channels), BF),
        back_one=vm((rows + 2, width, channels), BF),
        pre_one=vm((rows, width, channels), F32),
        pre_two=vm((rows, width, channels), F32),
        hw_all=vm((bins, heads, channels, bin_width), BF),
        hw_rows=vm((heads, total, channels), BF),
        hw_cols=vm((channels, heads * total), BF),
        head_grad=vm((rows, heads, total, width), BF),
        x=vm((rows, width, channels), BF),
        w1=vm((3, 3, channels, channels), BF),
        w2=vm((3, 3, channels, channels), BF),
        tg=vm((heads, rows, width), jnp.int32),
        load=dma((5,)),
        store=dma((6,)),
        loss_acc=vm((1, width), F32),
        act_turned=vm((rows, channels, width), BF),
        g_acc=vm((3 * channels, 3 * channels), F32),
        col_out=vm((3, 3, 2, rows, channels), F32),
        col_in=vm((3, 2, 4, rows, channels), F32),
        row_in=vm((3, 2, width, channels), BF),
        halo_send=dma((3, 10)),
        halo_recv=dma((3, 10)),
        hw_send=dma((2, 2, bins)),
        hw_recv=dma((2, 2, bins)),
    )
    for name, (first, second) in dict(early=(2 * bins + 5, 7), late=(5, 5)).items():
        tile = (qr, channels)
        s[name + "_part"] = vm((2, nq, first) + tile, BF)
        s[name + "_core"] = vm((nq, first) + tile, BF)
        s[name + "_half"] = vm((nq, first) + tile, BF)
        s[name + "_plane"] = vm((nq, first) + tile, BF)
        s[name + "_sum"] = vm((bins, second) + tile, BF)
        s[name + "_ring"] = vm((nz, second) + tile, BF)
        s[name + "_out"] = vm((2, nq, second) + tile, BF)
        s[name + "_send"] = dma((2 + 2 * nq + nz,))
        s[name + "_recv"] = dma((2 + 2 * nq + nz,))
    return s


class Place:
    def __init__(self, lat, lon, bins):
        self.__dict__.update(layout(lat, lon, bins))
        self.lat_size, self.lon_size, self.bin_size = lat, lon, bins
        self.lat, self.lon, self.bin = (lax.axis_index(a) for a in ("lat", "lon", "bin"))
        self.core = self.lat % CORES
        self.x = (self.lat // CORES) % self.nx
        self.zlo = self.lat // (CORES * self.nx)
        self.y = self.lon
        self.nq, self.nz = self.nx * self.ny, self.nzl * self.nzh
        self.z = self.bin * self.nzl + self.zlo
        self.q = self.x * self.ny + self.y
        self.row_block = self.lat * bins + self.bin
        self.row_blocks = lat * bins

    def device(self, lat=None, lon=None, bin=None):
        pick = lambda v, own: own if v is None else v
        return dict(lat=pick(lat, self.lat), lon=pick(lon, self.lon), bin=pick(bin, self.bin))

    def at(self, core=None, x=None, zlo=None):
        core = self.core if core is None else core
        x = self.x if x is None else x
        zlo = self.zlo if zlo is None else zlo
        return (zlo * self.nx + x) * CORES + core

    def partner(self):
        return self.device(lat=self.at(core=1 - self.core))

    def plane(self):
        for dx in range(self.nx):
            for dy in range(self.ny):
                if dx or dy:
                    x, y = (self.x + dx) % self.nx, (self.y + dy) % self.ny
                    yield dx * self.ny + dy, x * self.ny + y, self.device(lat=self.at(x=x), lon=y)

    def ring(self):
        for dz in range(1, self.nz):
            z = (self.z + dz) % self.nz
            zhi, zlo = z // self.nzl, z % self.nzl
            yield dz, zhi, self.device(lat=self.at(zlo=zlo), bin=zhi)

    def bins(self):
        if self.nzl == 2 and self.bin_size == 4:
            side = 2 * self.zlo - 1
            for step, other in ((1, True), (2, True), (1, False)):
                zlo = 1 - self.zlo if other else self.zlo
                to = (self.bin + step * side + 4) % 4
                source = (self.bin + (step if other else -step) * side + 4) % 4
                yield source, self.device(lat=self.at(zlo=zlo), bin=to)
        else:
            for step in range(1, self.bin_size):
                to = (self.bin + step) % self.bin_size
                yield (self.bin - step + self.bin_size) % self.bin_size, self.device(bin=to)

    def neighbour(self, down, right):
        block = (self.row_block + down) % self.row_blocks
        return self.device(
            lat=block // self.bin_size, lon=(self.lon + right) % self.lon_size, bin=block % self.bin_size
        )


NEIGHBOURS = [(-1, 0), (1, 0), (0, -1), (0, 1), (-1, -1), (-1, 1), (1, -1), (1, 1)]
EARLY = (8, 9)


def enter(place):
    barrier = pltpu.get_barrier_semaphore()
    peers = [place.neighbour(*n) for n in NEIGHBOURS]
    peers += [place.partner()]
    peers += [device for _, _, device in place.plane()]
    peers += [device for _, _, device in place.ring()]
    for device in peers:
        pl.semaphore_signal(barrier, inc=1, device_id=device, device_id_type=MESH)
    return len(peers)


def remote(src, dst, send, recv, device):
    copy = pltpu.make_async_remote_copy(
        src_ref=src, dst_ref=dst, send_sem=send, recv_sem=recv, device_id=device, device_id_type=MESH
    )
    copy.start()
    return copy


class Halo:
    def __init__(self, k, place, s):
        self.k, self.place, self.s = k, place, s
        self.rows, self.width, _ = s["act_one"].shape
        self.pitch = self.width + 16
        self.copies = {}

    def line(self, r):
        start = (r + 1) * self.pitch + 8
        return pl.ds(start if isinstance(r, int) else pl.multiple_of(start, 8), self.width)

    def column(self, c):
        return pl.ds(self.pitch + 8 + c, self.rows, stride=self.pitch)

    def go(self, i, src, dst):
        k, s = self.k, self.s
        self.copies[i] = remote(
            src, dst, s["halo_send"].at[k, i], s["halo_recv"].at[k, i], self.place.neighbour(*NEIGHBOURS[i - 6 if i in EARLY else i])
        )

    def send_rows(self, top, bottom):
        self.go(0, top, self.s["row_in"].at[self.k, 1])
        self.go(1, bottom, self.s["row_in"].at[self.k, 0])

    def send_columns(self, which, use):
        k, s, frame = self.k, self.s, self.s["frame"]
        s["col_out"][k, which, 0] = frame[self.column(0), :]
        s["col_out"][k, which, 1] = frame[self.column(self.width - 1), :]
        for i in use:
            down, right = NEIGHBOURS[i - 6 if i in EARLY else i]
            src = s["col_out"].at[k, which, 0 if right < 0 else 1]
            self.go(i, src, s["col_in"].at[k, 1 if right < 0 else 0, 3 if i in EARLY else 1 - down])

    def send_sides(self):
        self.send_columns(0, (2, 3))

    def send_early_sides(self):
        self.send_columns(2, EARLY)

    def send_corners(self):
        self.send_columns(1, (4, 5, 6, 7))

    def receive_sides(self, early=False):
        k, place, s, frame = self.k, self.place, self.s, self.s["frame"]
        for i in EARLY if early else (2, 3):
            self.copies[i].wait()
        for side, there, c in ((0, place.lon > 0, -1), (1, place.lon < place.lon_size - 1, self.width)):
            frame[self.column(c), :] = jnp.where(there, s["col_in"][k, side, 3 if early else 1], 0.0)

    def receive_rest(self):
        k, place, s, frame = self.k, self.place, self.s, self.s["frame"]
        for i in (0, 1, 4, 5, 6, 7):
            self.copies[i].wait()
        rows, width, pitch = self.rows, self.width, self.pitch
        up = place.row_block > 0
        down = place.row_block < place.row_blocks - 1
        frame[self.line(-1), :] = jnp.where(up, s["row_in"][k, 0].astype(F32), 0.0)
        frame[self.line(rows), :] = jnp.where(down, s["row_in"][k, 1].astype(F32), 0.0)
        for side, there, c in ((0, place.lon > 0, -1), (1, place.lon < place.lon_size - 1, width)):
            got = s["col_in"]
            frame[pl.ds(8 + c, 1), :] = jnp.where(
                there & up, got[k, side, 0, pl.ds(rows - 1, 1), :], 0.0
            )
            frame[pl.ds((rows + 1) * pitch + 8 + c, 1), :] = jnp.where(
                there & down, got[k, side, 2, pl.ds(0, 1), :], 0.0
            )


def fill_patches(frame, patches, first, count, step, width):
    pitch = width + 16

    def body(i, carry):
        r = first + i * step
        to = pl.multiple_of(r * width, width)
        for b in range(3):
            window = frame[pl.ds(r * pitch + 7 + b, width), :]
            patches[pl.ds(to, width), b * 128 : (b + 1) * 128] = window.astype(BF)
        return carry

    lax.fori_loop(0, count, body, 0)


def fix_patches(frame, patches, lines, width):
    pitch = width + 16
    for r in lines:
        patches[pl.ds(r * width, 16), :128] = frame[pl.ds(r * pitch + 7, 16), :].astype(BF)
        patches[pl.ds((r + 1) * width - 16, 16), 256:] = frame[
            pl.ds(r * pitch + width - 7, 16), :
        ].astype(BF)


def fill_weights(out, taps, channels):
    wide = 3 * channels
    out[pl.ds(3 * wide, wide), :channels] = jnp.zeros((wide, channels), BF)
    out[pl.ds(0, wide), channels:] = jnp.zeros((wide, channels), BF)
    for a in range(3):
        for b in range(3):
            tap = taps(a, b)
            for second in range(2):
                at = (a + second) * wide + b * channels
                out[at : at + channels, second * channels : (second + 1) * channels] = tap


def convolve(patches, weights, first, pairs, step, width, finish):
    def body(p, carry):
        r = first + p * step
        lines = [patches[pl.ds(pl.multiple_of((r + a) * width, width), width), :] for a in range(4)]
        both = dot(jnp.concatenate(lines, axis=1), weights[...])
        half = both.shape[1] // 2
        finish(r, both[:, :half])
        finish(r + 1, both[:, half:])
        return carry

    lax.fori_loop(0, pairs, body, 0)


def convolve_outer(patches, weights, rows, width, finish):
    wide, half = patches.shape[1], weights.shape[1] // 2

    def body(p, carry):
        r = p * (rows - 1)
        lines = [patches[pl.ds(pl.multiple_of((r + a) * width, width), width), :] for a in range(3)]
        finish(r, dot(jnp.concatenate(lines, axis=1), weights[: 3 * wide, :half]))
        return carry

    lax.fori_loop(0, 2, body, 0)


def kernel_grad(patches, upstream, acc, rows, width):
    channels = upstream.shape[2]
    upstream[0] = jnp.zeros((width, channels), BF)
    upstream[rows + 1] = jnp.zeros((width, channels), BF)
    group = rows // 2
    for g in range(2):
        left = patches[pl.ds((1 + g * group) * width, group * width), :]
        right = jnp.concatenate(
            [
                jnp.concatenate([upstream[1 + g * group + r + 1 - a] for a in range(3)], axis=1)
                for r in range(group)
            ],
            axis=0,
        )
        value = dot(left, right, ((0,), (0,)))
        if g == 0:
            acc[...] = value
        else:
            acc[...] += value
    acc[:, :channels] += dot(patches[pl.ds(0, width), :], upstream[1], ((0,), (0,)))
    acc[:, 2 * channels :] += dot(
        patches[pl.ds((rows + 1) * width, width), :], upstream[rows], ((0,), (0,))
    )


def joined(tile):
    total = jnp.sum(tile, axis=0, keepdims=True)
    high = total.astype(BF).astype(F32)
    row = lax.broadcasted_iota(jnp.int32, tile.shape, 0)
    return jnp.where(row == 0, high, jnp.where(row == 1, total - high, 0.0))


class Reduce:
    def __init__(self, name, place, s, heads=0):
        self.place, self.heads = place, heads
        for part in ("part", "core", "half", "plane", "sum", "ring", "out", "send", "recv"):
            setattr(self, part, s[name + "_" + part])
        self.sems = 0

    def go(self, src, dst, i, device):
        return remote(src, dst, self.send.at[i], self.recv.at[i], device)

    def rounded(self, value):
        if not self.heads:
            return value.astype(BF)
        last = jnp.where(self.place.core == 1, joined(value[-1]), value[-1])
        return jnp.concatenate([value[:-1], last[None]], axis=0).astype(BF)

    def step0(self):
        p = self.place
        self.copies = [self.go(self.part.at[1 - p.core], self.core, 0, p.partner())]

    def step1(self):
        p = self.place
        for copy in self.copies:
            copy.wait()

        def add(q):
            self.half[q] = self.rounded(self.part[p.core, q].astype(F32) + self.core[q].astype(F32))

        self.copies = []
        for d, q, device in p.plane():
            add(q)
            self.copies.append(self.go(self.half.at[q], self.plane.at[d], 1 + d, device))
        add(p.q)

    def step2(self):
        p = self.place
        for copy in self.copies:
            copy.wait()
        value = self.half[p.q].astype(F32)
        for d in range(1, p.nq):
            value = value + self.plane[d].astype(F32)
        value = self.rounded(value)
        if self.heads:
            for b in range(p.bin_size):
                own = value[2 * b : 2 * b + 2]
                self.sum[b] = jnp.concatenate([own, value[self.heads :]], axis=0)
        else:
            self.sum[0] = value
        mine = p.bin if self.heads else 0
        self.ring[p.z] = self.sum[mine]
        self.copies = [
            self.go(self.sum.at[zhi if self.heads else 0], self.ring.at[p.z], 1 + p.nq + dz, device)
            for dz, zhi, device in p.ring()
        ]

    def step3(self):
        p = self.place
        for copy in self.copies:
            copy.wait()
        value = self.ring[0].astype(F32)
        for z in range(1, p.nz):
            value = value + self.ring[z].astype(F32)
        self.out[p.core, p.q] = self.rounded(value)
        mine = self.out.at[p.core, p.q]
        base = 1 + p.nq + p.nz
        self.copies = [self.go(mine, mine, base + d, device) for d, _, device in p.plane()]

    def step4(self):
        p = self.place
        for copy in self.copies:
            copy.wait()
        mine = self.out.at[p.core]
        self.copies = [self.go(mine, mine, 1 + 2 * p.nq + p.nz, p.partner())]

    def step5(self):
        for copy in self.copies:
            copy.wait()


def pack_grad(acc, part, channels, first=0):
    qr = part.shape[-2]
    for a in range(3):
        for b in range(3):
            c, t = divmod(3 * a + b, 5)
            tap = acc[b * channels : (b + 1) * channels, a * channels : (a + 1) * channels]
            part[c, :, first + t] = tap.reshape(channels // qr, qr, channels).astype(BF)


def unpack_grad(out, result, channels, first=0):
    for a in range(3):
        for b in range(3):
            c, t = divmod(3 * a + b, 5)
            result[a, b] = out[c, :, first + t].astype(F32).reshape(channels, channels)


def turned(tile):
    return jnp.transpose(tile.astype(F32)).astype(BF)


def load(src, dst, sem):
    copy = pltpu.make_async_copy(src, dst, sem)
    copy.start()
    return copy


def kernel(sizes, names, x_ref, w1_ref, w2_ref, hw_ref, tg_ref, late_ref, early_ref, *refs):
    lat, lon, bins, cells_all = sizes
    s = dict(zip(names, refs))
    place = Place(lat, lon, bins)
    rows, width, channels = x_ref.shape
    heads, total, _ = s["hw_rows"].shape
    bin_width = total // bins
    half_heads = heads // 2
    frame, hw_all = s["frame"], s["hw_all"]
    scale = 1.0 / math.sqrt(heads * cells_all)

    peers = enter(place)
    loads = [
        load(x_ref, s["x"], s["load"].at[0]),
        load(w1_ref, s["w1"], s["load"].at[1]),
        load(w2_ref, s["w2"], s["load"].at[2]),
        load(hw_ref, hw_all.at[place.bin], s["load"].at[3]),
        load(tg_ref.at[:, pl.ds(place.bin * rows, rows), :], s["tg"], s["load"].at[4]),
    ]
    pl.semaphore_wait(pltpu.get_barrier_semaphore(), peers)

    halo = Halo(0, place, s)
    own_first = place.core * half_heads
    hw_copies = [[], []]
    sources = [source for source, _ in place.bins()]

    def send_head(kk):
        k = own_first + kk
        for j, (_, device) in enumerate(place.bins()):
            hw_copies[kk].append(
                remote(
                    hw_ref.at[k],
                    hw_all.at[place.bin, k],
                    s["hw_send"].at[0, kk, j],
                    s["hw_recv"].at[0, kk, j],
                    device,
                )
            )

    forwards = [[], []]

    def forward_head(kk):
        for j, source in enumerate(sources):
            hw_copies[kk][j].wait()
            there = hw_all.at[source, own_first + kk]
            forwards[kk].append(
                remote(
                    there, there, s["hw_send"].at[1, kk, j], s["hw_recv"].at[1, kk, j], place.partner()
                )
            )

    send_head(0)
    halo.send_rows(x_ref.at[0], x_ref.at[rows - 1])
    loads[0].wait()
    for r in range(rows):
        frame[halo.line(r), :] = s["x"][r].astype(F32)
    halo.send_sides()
    halo.send_corners()
    send_head(1)

    fill_patches(frame, s["px"], 1, rows, 1, width)
    loads[1].wait()
    fill_weights(s["w_one"], lambda a, b: s["w1"][a, b], channels)
    halo.receive_sides()
    fix_patches(frame, s["px"], range(1, rows + 1), width)

    def finish_one(r, value):
        s["pre_one"][r] = value
        act = jnp.maximum(value, 0.0).astype(BF)
        s["act_one"][r] = act
        frame[halo.line(r), :] = act.astype(F32)

    convolve(s["px"], s["w_one"], 1, (rows - 2) // 2, 2, width, finish_one)
    next_halo = Halo(1, place, s)
    next_halo.send_early_sides()
    loads[2].wait()
    fill_weights(s["w_two"], lambda a, b: s["w2"][a, b], channels)
    fill_weights(s["w_flip"], lambda a, b: turned(s["w2"][2 - a, 2 - b]), channels)
    halo.receive_rest()
    fill_patches(frame, s["px"], 0, 2, rows + 1, width)
    convolve_outer(s["px"], s["w_one"], rows, width, finish_one)
    halo = next_halo
    halo.send_sides()
    halo.send_rows(s["act_one"].at[0], s["act_one"].at[rows - 1])
    halo.send_corners()

    fill_patches(frame, s["pa"], 1, rows, 1, width)
    halo.receive_sides(early=True)
    fix_patches(frame, s["pa"], range(1, rows + 1), width)

    def finish_two(r, value):
        s["pre_two"][r] = value
        act = jnp.maximum(value, 0.0).astype(BF)
        s["act_two"][r] = act
        s["act_turned"][r] = turned(act)

    convolve(s["pa"], s["w_two"], 2, (rows - 4) // 2, 2, width, finish_two)

    for copy in loads[3:]:
        copy.wait()
    hw_rows, hw_cols = s["hw_rows"], s["hw_cols"]
    s["loss_acc"][...] = jnp.zeros_like(s["loss_acc"])
    last_halo = Halo(2, place, s)

    def prepare_head(k):
        for b in range(bins):
            tile = hw_all[b, k]
            start = k * total + b * bin_width
            hw_cols[:, pl.ds(pl.multiple_of(start, 128), bin_width)] = tile
            hw_rows[k, b * bin_width : (b + 1) * bin_width, :] = turned(tile)

    def head_unit(k, pair):
        eight = lax.broadcasted_iota(jnp.int32, (8, width), 0)
        group = lax.broadcasted_iota(jnp.int32, (total // 8, 8, width), 0)
        loss = s["loss_acc"][...]
        logits = [dot(hw_rows[k], s["act_turned"][r]).reshape(total // 8, 8, width) for r in pair]
        for r, value in zip(pair, logits):
            highest = jnp.max(jnp.max(value, axis=0), axis=0, keepdims=True)
            raised = jnp.exp(value - highest[None])
            summed = jnp.sum(jnp.sum(raised, axis=0), axis=0, keepdims=True)
            label = s["tg"][k, pl.ds(r, 1), :] - eight
            chosen = group * 8 == label[None]
            picked = jnp.sum(jnp.sum(jnp.where(chosen, value, 0.0), axis=0), axis=0, keepdims=True)
            loss = loss + (highest + jnp.log(summed) - picked)
            prob = raised * (scale / summed)[None]
            grad = jnp.where(chosen, prob - scale, prob).reshape(total, width).astype(BF)
            s["head_grad"][r, k] = grad
        s["loss_acc"][...] = loss

    def head_row(r):
        eight = lax.broadcasted_iota(jnp.int32, (8, width), 0)
        group = lax.broadcasted_iota(jnp.int32, (total // 8, 8, width), 0)
        loss = s["loss_acc"][...]
        back = jnp.zeros((channels, width), F32)
        for k in range(heads):
            value = dot(hw_rows[k], s["act_turned"][r]).reshape(total // 8, 8, width)
            highest = jnp.max(jnp.max(value, axis=0), axis=0, keepdims=True)
            raised = jnp.exp(value - highest[None])
            summed = jnp.sum(jnp.sum(raised, axis=0), axis=0, keepdims=True)
            label = s["tg"][k, pl.ds(r, 1), :] - eight
            chosen = group * 8 == label[None]
            picked = jnp.sum(jnp.sum(jnp.where(chosen, value, 0.0), axis=0), axis=0, keepdims=True)
            loss = loss + (highest + jnp.log(summed) - picked)
            prob = raised * (scale / summed)[None]
            grad = jnp.where(chosen, prob - scale, prob).reshape(total, width).astype(BF)
            s["head_grad"][r, k] = grad
            back = back + dot(hw_cols[:, k * total : (k + 1) * total], grad)
        s["loss_acc"][...] = loss
        finish_heads(r, back)

    def finish_heads(r, back):
        hidden = jnp.where(s["pre_two"][r] > 0, jnp.transpose(back), 0.0).astype(BF)
        s["back_two"][r + 1] = hidden
        frame[halo.line(r), :] = hidden.astype(F32)

    def loop(count, body):
        lax.fori_loop(0, count, lambda i, carry: (body(i), carry)[1], 0)

    for kk in range(heads):
        k = (own_first + kk) % heads
        if kk < half_heads:
            forward_head(kk)
        else:
            for copy in forwards[kk - half_heads]:
                copy.wait()
        prepare_head(k)
        loop((rows - 4) // 2, lambda i: head_unit(k, (2 + 2 * i, 3 + 2 * i)))
    def finish_inner(r):
        grads = s["head_grad"][r].reshape(heads * total, width)
        finish_heads(r, dot(hw_cols[...], grads))

    loop(rows - 4, lambda i: finish_inner(2 + i))
    halo.receive_sides()
    fix_patches(frame, s["pa"], (1, rows), width)
    halo.receive_rest()
    fill_patches(frame, s["pa"], 0, 2, rows + 1, width)
    convolve(s["pa"], s["w_two"], 0, 2, rows - 2, width, finish_two)
    loop(2, lambda i: head_row((rows - 1) * i))
    last_halo.send_rows(s["back_two"].at[1], s["back_two"].at[rows])
    last_halo.send_corners()
    loop(2, lambda i: head_row(1 + (rows - 3) * i))
    last_halo.send_sides()
    halo = last_halo

    early = Reduce("early", place, s, heads=2 * bins)
    late = Reduce("late", place, s)
    qr = early.part.shape[-2]
    feats = s["act_two"][...].reshape(rows * width, channels)
    for k in range(heads):
        c, kk = divmod(k, half_heads)
        grads = jnp.concatenate([s["head_grad"][r, k] for r in range(rows)], axis=1)
        value = dot(grads, feats).reshape(bins, bin_width // qr, qr, channels)
        for b in range(bins):
            early.part[c, :, 2 * b + kk] = value[b].astype(BF)
    kernel_grad(s["pa"], s["back_two"], s["g_acc"], rows, width)
    pack_grad(s["g_acc"], early.part, channels, 2 * bins)
    loss = s["loss_acc"][...]
    lanes = loss[:, :128]
    for i in range(1, width // 128):
        lanes = lanes + loss[:, i * 128 : (i + 1) * 128]
    row = lax.broadcasted_iota(jnp.int32, (qr, 128), 0)
    loss_tile = joined(jnp.where(row == 0, lanes, 0.0)).astype(BF)
    for q in range(place.nq):
        early.part[1, q, 2 * bins + 4] = loss_tile
        late.part[1, q, 4] = jnp.zeros((qr, channels), BF)
    early.step0()

    fill_patches(frame, s["pg"], 1, rows, 1, width)
    halo.receive_sides()
    fix_patches(frame, s["pg"], range(1, rows + 1), width)
    halo.receive_rest()
    fill_patches(frame, s["pg"], 0, 2, rows + 1, width)

    def finish_back(r, value):
        s["back_one"][r + 1] = jnp.where(s["pre_one"][r] > 0, value, 0.0).astype(BF)

    convolve(s["pg"], s["w_flip"], 0, rows // 2, 2, width, finish_back)
    early.step1()
    kernel_grad(s["px"], s["back_one"], s["g_acc"], rows, width)
    pack_grad(s["g_acc"], late.part, channels)
    late.step0()
    late.step1()
    early.step2()
    late.step2()
    early.step3()
    late.step3()
    early.step4()
    early.step5()
    stores = [load(early.out, early_ref, s["store"].at[0])]
    late.step4()
    stores.append(load(late.out.at[place.core], late_ref.at[place.core], s["store"].at[1]))
    late.step5()
    other = 1 - place.core
    stores.append(load(late.out.at[other], late_ref.at[other], s["store"].at[2]))
    for copy in stores:
        copy.wait()


def unpack(count, late_hbm, early_hbm, loss_ref, g1_hbm, g2_hbm, gh_hbm, *scratch):
    late_in, early_in, g1, g2, gh, sems = scratch
    heads, channels, bin_width = gh.shape
    loads = [load(early_hbm, early_in, sems.at[0]), load(late_hbm, late_in, sems.at[1])]
    loads[0].wait()
    unpack_grad(early_in, g2, channels, 2)
    stores = [load(g2, g2_hbm, sems.at[2])]
    loads[1].wait()
    unpack_grad(late_in, g1, channels)
    stores.append(load(g1, g1_hbm, sems.at[3]))
    for k in range(heads):
        c, kk = divmod(k, heads // 2)
        gh[k] = jnp.transpose(early_in[c, :, kk].astype(F32).reshape(bin_width, channels))
    stores.append(load(gh, gh_hbm, sems.at[4]))
    whole = jnp.sum(early_in[1, 0, 6].astype(F32), axis=0, keepdims=True)
    loss_ref[...] = jnp.sum(whole, axis=1, keepdims=True) * (1.0 / count)
    for copy in stores:
        copy.wait()


def per_device(inputs, conv_one, conv_two, head_weight, targets):
    rows, width, channels = inputs.shape
    heads, _, bin_width = head_weight.shape
    lat, lon, bins = (lax.axis_size(a) for a in ("lat", "lon", "bin"))
    cells_all = rows * lat * bins * width * lon
    scratch = plan(lat, lon, bins, rows, width, channels, heads, bin_width)
    vmem = pl.BlockSpec(memory_space=pltpu.VMEM)
    hbm = pl.BlockSpec(memory_space=pl.ANY)
    parts = pl.pallas_call(
        functools.partial(kernel, (lat, lon, bins, cells_all), tuple(scratch)),
        out_shape=[
            jax.ShapeDtypeStruct(scratch[name + "_out"].shape, BF) for name in ("late", "early")
        ],
        in_specs=[hbm] * 5,
        out_specs=[hbm] * 2,
        scratch_shapes=list(scratch.values()),
        compiler_params=pltpu.CompilerParams(
            collective_id=0, has_side_effects=True, vmem_limit_bytes=60 << 20
        ),
    )(inputs, conv_one, conv_two, head_weight, targets)
    loss, g1, g2, gh = pl.pallas_call(
        functools.partial(unpack, heads * cells_all),
        out_shape=[
            jax.ShapeDtypeStruct((1, 1), F32),
            jax.ShapeDtypeStruct(conv_one.shape, F32),
            jax.ShapeDtypeStruct(conv_two.shape, F32),
            jax.ShapeDtypeStruct(head_weight.shape, F32),
        ],
        in_specs=[hbm] * 2,
        out_specs=[vmem] + [hbm] * 3,
        scratch_shapes=[
            pltpu.VMEM(scratch["late_out"].shape, BF),
            pltpu.VMEM(scratch["early_out"].shape, BF),
            pltpu.VMEM(conv_one.shape, F32),
            pltpu.VMEM(conv_two.shape, F32),
            pltpu.VMEM(head_weight.shape, F32),
            pltpu.SemaphoreType.DMA((5,)),
        ],
    )(*parts)
    return (loss.reshape(()), g1, g2, gh)


def solution(mesh):
    in_specs = (
        P(("lat", "bin"), "lon", None),
        P(),
        P(),
        P(None, None, "bin"),
        P(None, "lat", "lon"),
    )
    out_specs = (P(), P(), P(), P(None, None, "bin"))
    return jax.shard_map(
        per_device, mesh=mesh, in_specs=in_specs, out_specs=out_specs, check_vma=False
    )
```

```python
import functools
import math

import jax
import jax.numpy as jnp
from jax import lax
from jax.experimental import pallas as pl
from jax.experimental.pallas import tpu as pltpu
from jax.sharding import PartitionSpec as P

BF = jnp.bfloat16
F32 = jnp.float32
MESH = pl.DeviceIdType.MESH
CORES = 2
PLANE_X = 4


def dot(left, right, contract=((1,), (0,))):
    return lax.dot_general(left, right, (contract, ((), ())), preferred_element_type=F32)


def layout(lat, lon, bins):
    plane_x = min(PLANE_X, lat // CORES)
    return dict(nx=plane_x, nzl=lat // (CORES * plane_x), ny=lon, nzh=bins)


def plan(lat, lon, bins, rows, width, channels, heads, bin_width):
    d = layout(lat, lon, bins)
    nq, nz = d["nx"] * d["ny"], d["nzl"] * d["nzh"]
    qr = channels // nq
    pitch = width + 16
    total = bins * bin_width
    vm, dma = pltpu.VMEM, pltpu.SemaphoreType.DMA
    s = dict(
        frame=vm(((rows + 2) * pitch, channels), F32),
        px=vm(((rows + 2) * width, 3 * channels), BF),
        pa=vm(((rows + 2) * width, 3 * channels), BF),
        pg=vm(((rows + 2) * width, 3 * channels), BF),
        w_one=vm((12 * channels, 2 * channels), BF),
        w_two=vm((12 * channels, 2 * channels), BF),
        w_flip=vm((12 * channels, 2 * channels), BF),
        act_one=vm((rows, width, channels), BF),
        act_two=vm((rows, width, channels), BF),
        back_two=vm((rows + 2, width, channels), BF),
        back_one=vm((rows + 2, width, channels), BF),
        pre_one=vm((rows, width, channels), F32),
        pre_two=vm((rows, width, channels), F32),
        hw_all=vm((bins, heads, channels, bin_width), BF),
        hw_rows=vm((heads, total, channels), BF),
        hw_cols=vm((channels, heads * total), BF),
        head_grad=vm((rows, heads, total, width), BF),
        x=vm((rows, width, channels), BF),
        w1=vm((3, 3, channels, channels), BF),
        w2=vm((3, 3, channels, channels), BF),
        tg=vm((heads, rows, width), jnp.int32),
        load=dma((5,)),
        store=dma((6,)),
        loss_acc=vm((1, width), F32),
        act_turned=vm((rows, channels, width), BF),
        g_acc=vm((3 * channels, 3 * channels), F32),
        col_out=vm((3, 3, 2, rows, channels), F32),
        col_in=vm((3, 2, 4, rows, channels), F32),
        row_in=vm((3, 2, width, channels), BF),
        halo_send=dma((3, 10)),
        halo_recv=dma((3, 10)),
        hw_send=dma((2, 2, bins)),
        hw_recv=dma((2, 2, bins)),
    )
    for name, (first, second) in dict(early=(2 * bins + 5, 7), late=(5, 5)).items():
        tile = (qr, channels)
        s[name + "_part"] = vm((2, nq, first) + tile, BF)
        s[name + "_core"] = vm((nq, first) + tile, BF)
        s[name + "_half"] = vm((nq, first) + tile, BF)
        s[name + "_plane"] = vm((nq, first) + tile, BF)
        s[name + "_sum"] = vm((bins, second) + tile, BF)
        s[name + "_ring"] = vm((nz, second) + tile, BF)
        s[name + "_out"] = vm((2, nq, second) + tile, BF)
        s[name + "_send"] = dma((2 + 2 * nq + nz,))
        s[name + "_recv"] = dma((2 + 2 * nq + nz,))
    return s


class Place:
    def __init__(self, lat, lon, bins):
        self.__dict__.update(layout(lat, lon, bins))
        self.lat_size, self.lon_size, self.bin_size = lat, lon, bins
        self.lat, self.lon, self.bin = (lax.axis_index(a) for a in ("lat", "lon", "bin"))
        self.core = self.lat % CORES
        self.x = (self.lat // CORES) % self.nx
        self.zlo = self.lat // (CORES * self.nx)
        self.y = self.lon
        self.nq, self.nz = self.nx * self.ny, self.nzl * self.nzh
        self.z = self.bin * self.nzl + self.zlo
        self.q = self.x * self.ny + self.y
        self.row_block = self.lat * bins + self.bin
        self.row_blocks = lat * bins

    def device(self, lat=None, lon=None, bin=None):
        pick = lambda v, own: own if v is None else v
        return dict(lat=pick(lat, self.lat), lon=pick(lon, self.lon), bin=pick(bin, self.bin))

    def at(self, core=None, x=None, zlo=None):
        core = self.core if core is None else core
        x = self.x if x is None else x
        zlo = self.zlo if zlo is None else zlo
        return (zlo * self.nx + x) * CORES + core

    def partner(self):
        return self.device(lat=self.at(core=1 - self.core))

    def plane(self):
        for dx in range(self.nx):
            for dy in range(self.ny):
                if dx or dy:
                    x, y = (self.x + dx) % self.nx, (self.y + dy) % self.ny
                    yield dx * self.ny + dy, x * self.ny + y, self.device(lat=self.at(x=x), lon=y)

    def ring(self):
        for dz in range(1, self.nz):
            z = (self.z + dz) % self.nz
            zhi, zlo = z // self.nzl, z % self.nzl
            yield dz, zhi, self.device(lat=self.at(zlo=zlo), bin=zhi)

    def bins(self):
        if self.nzl == 2 and self.bin_size == 4:
            side = 2 * self.zlo - 1
            for step, other in ((1, True), (2, True), (1, False)):
                zlo = 1 - self.zlo if other else self.zlo
                to = (self.bin + step * side + 4) % 4
                source = (self.bin + (step if other else -step) * side + 4) % 4
                yield source, self.device(lat=self.at(zlo=zlo), bin=to)
        else:
            for step in range(1, self.bin_size):
                to = (self.bin + step) % self.bin_size
                yield (self.bin - step + self.bin_size) % self.bin_size, self.device(bin=to)

    def neighbour(self, down, right):
        block = (self.row_block + down) % self.row_blocks
        return self.device(
            lat=block // self.bin_size, lon=(self.lon + right) % self.lon_size, bin=block % self.bin_size
        )


NEIGHBOURS = [(-1, 0), (1, 0), (0, -1), (0, 1), (-1, -1), (-1, 1), (1, -1), (1, 1)]
EARLY = (8, 9)


def enter(place):
    barrier = pltpu.get_barrier_semaphore()
    peers = [place.neighbour(*n) for n in NEIGHBOURS]
    peers += [place.partner()]
    peers += [device for _, _, device in place.plane()]
    peers += [device for _, _, device in place.ring()]
    for device in peers:
        pl.semaphore_signal(barrier, inc=1, device_id=device, device_id_type=MESH)
    return len(peers)


def remote(src, dst, send, recv, device):
    copy = pltpu.make_async_remote_copy(
        src_ref=src, dst_ref=dst, send_sem=send, recv_sem=recv, device_id=device, device_id_type=MESH
    )
    copy.start()
    return copy


class Halo:
    def __init__(self, k, place, s):
        self.k, self.place, self.s = k, place, s
        self.rows, self.width, _ = s["act_one"].shape
        self.pitch = self.width + 16
        self.copies = {}

    def line(self, r):
        start = (r + 1) * self.pitch + 8
        return pl.ds(start if isinstance(r, int) else pl.multiple_of(start, 8), self.width)

    def column(self, c):
        return pl.ds(self.pitch + 8 + c, self.rows, stride=self.pitch)

    def go(self, i, src, dst):
        k, s = self.k, self.s
        self.copies[i] = remote(
            src, dst, s["halo_send"].at[k, i], s["halo_recv"].at[k, i], self.place.neighbour(*NEIGHBOURS[i - 6 if i in EARLY else i])
        )

    def send_rows(self, top, bottom):
        self.go(0, top, self.s["row_in"].at[self.k, 1])
        self.go(1, bottom, self.s["row_in"].at[self.k, 0])

    def send_columns(self, which, use):
        k, s, frame = self.k, self.s, self.s["frame"]
        s["col_out"][k, which, 0] = frame[self.column(0), :]
        s["col_out"][k, which, 1] = frame[self.column(self.width - 1), :]
        for i in use:
            down, right = NEIGHBOURS[i - 6 if i in EARLY else i]
            src = s["col_out"].at[k, which, 0 if right < 0 else 1]
            self.go(i, src, s["col_in"].at[k, 1 if right < 0 else 0, 3 if i in EARLY else 1 - down])

    def send_sides(self):
        self.send_columns(0, (2, 3))

    def send_early_sides(self):
        self.send_columns(2, EARLY)

    def send_corners(self):
        self.send_columns(1, (4, 5, 6, 7))

    def receive_sides(self, early=False):
        k, place, s, frame = self.k, self.place, self.s, self.s["frame"]
        for i in EARLY if early else (2, 3):
            self.copies[i].wait()
        for side, there, c in ((0, place.lon > 0, -1), (1, place.lon < place.lon_size - 1, self.width)):
            frame[self.column(c), :] = jnp.where(there, s["col_in"][k, side, 3 if early else 1], 0.0)

    def receive_rest(self):
        k, place, s, frame = self.k, self.place, self.s, self.s["frame"]
        for i in (0, 1, 4, 5, 6, 7):
            self.copies[i].wait()
        rows, width, pitch = self.rows, self.width, self.pitch
        up = place.row_block > 0
        down = place.row_block < place.row_blocks - 1
        frame[self.line(-1), :] = jnp.where(up, s["row_in"][k, 0].astype(F32), 0.0)
        frame[self.line(rows), :] = jnp.where(down, s["row_in"][k, 1].astype(F32), 0.0)
        for side, there, c in ((0, place.lon > 0, -1), (1, place.lon < place.lon_size - 1, width)):
            got = s["col_in"]
            frame[pl.ds(8 + c, 1), :] = jnp.where(
                there & up, got[k, side, 0, pl.ds(rows - 1, 1), :], 0.0
            )
            frame[pl.ds((rows + 1) * pitch + 8 + c, 1), :] = jnp.where(
                there & down, got[k, side, 2, pl.ds(0, 1), :], 0.0
            )


def fill_patches(frame, patches, first, count, step, width):
    pitch = width + 16

    def body(i, carry):
        r = first + i * step
        to = pl.multiple_of(r * width, width)
        for b in range(3):
            window = frame[pl.ds(r * pitch + 7 + b, width), :]
            patches[pl.ds(to, width), b * 128 : (b + 1) * 128] = window.astype(BF)
        return carry

    lax.fori_loop(0, count, body, 0)


def fix_patches(frame, patches, lines, width):
    pitch = width + 16
    for r in lines:
        patches[pl.ds(r * width, 16), :128] = frame[pl.ds(r * pitch + 7, 16), :].astype(BF)
        patches[pl.ds((r + 1) * width - 16, 16), 256:] = frame[
            pl.ds(r * pitch + width - 7, 16), :
        ].astype(BF)


def fill_weights(out, taps, channels):
    wide = 3 * channels
    out[pl.ds(3 * wide, wide), :channels] = jnp.zeros((wide, channels), BF)
    out[pl.ds(0, wide), channels:] = jnp.zeros((wide, channels), BF)
    for a in range(3):
        for b in range(3):
            tap = taps(a, b)
            for second in range(2):
                at = (a + second) * wide + b * channels
                out[at : at + channels, second * channels : (second + 1) * channels] = tap


def convolve(patches, weights, first, pairs, step, width, finish):
    def body(p, carry):
        r = first + p * step
        lines = [patches[pl.ds(pl.multiple_of((r + a) * width, width), width), :] for a in range(4)]
        both = dot(jnp.concatenate(lines, axis=1), weights[...])
        half = both.shape[1] // 2
        finish(r, both[:, :half])
        finish(r + 1, both[:, half:])
        return carry

    lax.fori_loop(0, pairs, body, 0)


def convolve_outer(patches, weights, rows, width, finish):
    wide, half = patches.shape[1], weights.shape[1] // 2

    def body(p, carry):
        r = p * (rows - 1)
        lines = [patches[pl.ds(pl.multiple_of((r + a) * width, width), width), :] for a in range(3)]
        finish(r, dot(jnp.concatenate(lines, axis=1), weights[: 3 * wide, :half]))
        return carry

    lax.fori_loop(0, 2, body, 0)


def kernel_grad(patches, upstream, acc, rows, width):
    channels = upstream.shape[2]
    upstream[0] = jnp.zeros((width, channels), BF)
    upstream[rows + 1] = jnp.zeros((width, channels), BF)
    group = rows // 2
    for g in range(2):
        left = patches[pl.ds((1 + g * group) * width, group * width), :]
        right = jnp.concatenate(
            [
                jnp.concatenate([upstream[1 + g * group + r + 1 - a] for a in range(3)], axis=1)
                for r in range(group)
            ],
            axis=0,
        )
        value = dot(left, right, ((0,), (0,)))
        if g == 0:
            acc[...] = value
        else:
            acc[...] += value
    acc[:, :channels] += dot(patches[pl.ds(0, width), :], upstream[1], ((0,), (0,)))
    acc[:, 2 * channels :] += dot(
        patches[pl.ds((rows + 1) * width, width), :], upstream[rows], ((0,), (0,))
    )


def joined(tile):
    total = jnp.sum(tile, axis=0, keepdims=True)
    high = total.astype(BF).astype(F32)
    row = lax.broadcasted_iota(jnp.int32, tile.shape, 0)
    return jnp.where(row == 0, high, jnp.where(row == 1, total - high, 0.0))


class Reduce:
    def __init__(self, name, place, s, heads=0):
        self.place, self.heads = place, heads
        for part in ("part", "core", "half", "plane", "sum", "ring", "out", "send", "recv"):
            setattr(self, part, s[name + "_" + part])
        self.sems = 0

    def go(self, src, dst, i, device):
        return remote(src, dst, self.send.at[i], self.recv.at[i], device)

    def rounded(self, value):
        if not self.heads:
            return value.astype(BF)
        last = jnp.where(self.place.core == 1, joined(value[-1]), value[-1])
        return jnp.concatenate([value[:-1], last[None]], axis=0).astype(BF)

    def step0(self):
        p = self.place
        self.copies = [self.go(self.part.at[1 - p.core], self.core, 0, p.partner())]

    def step1(self):
        p = self.place
        for copy in self.copies:
            copy.wait()

        def add(q):
            self.half[q] = self.rounded(self.part[p.core, q].astype(F32) + self.core[q].astype(F32))

        self.copies = []
        for d, q, device in p.plane():
            add(q)
            self.copies.append(self.go(self.half.at[q], self.plane.at[d], 1 + d, device))
        add(p.q)

    def step2(self):
        p = self.place
        for copy in self.copies:
            copy.wait()
        value = self.half[p.q].astype(F32)
        for d in range(1, p.nq):
            value = value + self.plane[d].astype(F32)
        value = self.rounded(value)
        if self.heads:
            for b in range(p.bin_size):
                own = value[2 * b : 2 * b + 2]
                self.sum[b] = jnp.concatenate([own, value[self.heads :]], axis=0)
        else:
            self.sum[0] = value
        mine = p.bin if self.heads else 0
        self.ring[p.z] = self.sum[mine]
        self.copies = [
            self.go(self.sum.at[zhi if self.heads else 0], self.ring.at[p.z], 1 + p.nq + dz, device)
            for dz, zhi, device in p.ring()
        ]

    def step3(self):
        p = self.place
        for copy in self.copies:
            copy.wait()
        value = self.ring[0].astype(F32)
        for z in range(1, p.nz):
            value = value + self.ring[z].astype(F32)
        self.out[p.core, p.q] = self.rounded(value)
        mine = self.out.at[p.core, p.q]
        base = 1 + p.nq + p.nz
        self.copies = [self.go(mine, mine, base + d, device) for d, _, device in p.plane()]

    def step4(self):
        p = self.place
        for copy in self.copies:
            copy.wait()
        mine = self.out.at[p.core]
        self.copies = [self.go(mine, mine, 1 + 2 * p.nq + p.nz, p.partner())]

    def step5(self):
        for copy in self.copies:
            copy.wait()


def pack_grad(acc, part, channels, first=0):
    qr = part.shape[-2]
    for a in range(3):
        for b in range(3):
            c, t = divmod(3 * a + b, 5)
            tap = acc[b * channels : (b + 1) * channels, a * channels : (a + 1) * channels]
            part[c, :, first + t] = tap.reshape(channels // qr, qr, channels).astype(BF)


def unpack_grad(out, result, channels, first=0):
    for a in range(3):
        for b in range(3):
            c, t = divmod(3 * a + b, 5)
            result[a, b] = out[c, :, first + t].astype(F32).reshape(channels, channels)


def turned(tile):
    return jnp.transpose(tile.astype(F32)).astype(BF)


def load(src, dst, sem):
    copy = pltpu.make_async_copy(src, dst, sem)
    copy.start()
    return copy


def kernel(sizes, names, x_ref, w1_ref, w2_ref, hw_ref, tg_ref, late_ref, early_ref, *refs):
    lat, lon, bins, cells_all = sizes
    s = dict(zip(names, refs))
    place = Place(lat, lon, bins)
    rows, width, channels = x_ref.shape
    heads, total, _ = s["hw_rows"].shape
    bin_width = total // bins
    half_heads = heads // 2
    frame, hw_all = s["frame"], s["hw_all"]
    scale = 1.0 / math.sqrt(heads * cells_all)

    peers = enter(place)
    loads = [
        load(x_ref, s["x"], s["load"].at[0]),
        load(w1_ref, s["w1"], s["load"].at[1]),
        load(w2_ref, s["w2"], s["load"].at[2]),
        load(hw_ref, hw_all.at[place.bin], s["load"].at[3]),
        load(tg_ref.at[:, pl.ds(place.bin * rows, rows), :], s["tg"], s["load"].at[4]),
    ]
    pl.semaphore_wait(pltpu.get_barrier_semaphore(), peers)

    halo = Halo(0, place, s)
    own_first = place.core * half_heads
    hw_copies = [[], []]
    sources = [source for source, _ in place.bins()]

    def send_head(kk):
        k = own_first + kk
        for j, (_, device) in enumerate(place.bins()):
            hw_copies[kk].append(
                remote(
                    hw_ref.at[k],
                    hw_all.at[place.bin, k],
                    s["hw_send"].at[0, kk, j],
                    s["hw_recv"].at[0, kk, j],
                    device,
                )
            )

    forwards = [[], []]

    def forward_head(kk):
        for j, source in enumerate(sources):
            hw_copies[kk][j].wait()
            there = hw_all.at[source, own_first + kk]
            forwards[kk].append(
                remote(
                    there, there, s["hw_send"].at[1, kk, j], s["hw_recv"].at[1, kk, j], place.partner()
                )
            )

    halo.send_rows(x_ref.at[0], x_ref.at[rows - 1])
    send_head(0)
    loads[0].wait()
    for r in range(rows):
        frame[halo.line(r), :] = s["x"][r].astype(F32)
    halo.send_sides()
    halo.send_corners()

    fill_patches(frame, s["px"], 1, rows, 1, width)
    loads[1].wait()
    fill_weights(s["w_one"], lambda a, b: s["w1"][a, b], channels)
    halo.receive_sides()
    fix_patches(frame, s["px"], range(1, rows + 1), width)

    def finish_one(r, value):
        s["pre_one"][r] = value
        act = jnp.maximum(value, 0.0).astype(BF)
        s["act_one"][r] = act
        frame[halo.line(r), :] = act.astype(F32)

    convolve(s["px"], s["w_one"], 1, (rows - 2) // 2, 2, width, finish_one)
    next_halo = Halo(1, place, s)
    next_halo.send_early_sides()
    send_head(1)
    loads[2].wait()
    fill_weights(s["w_two"], lambda a, b: s["w2"][a, b], channels)
    fill_weights(s["w_flip"], lambda a, b: turned(s["w2"][2 - a, 2 - b]), channels)
    halo.receive_rest()
    fill_patches(frame, s["px"], 0, 2, rows + 1, width)
    convolve_outer(s["px"], s["w_one"], rows, width, finish_one)
    halo = next_halo
    halo.send_sides()
    halo.send_rows(s["act_one"].at[0], s["act_one"].at[rows - 1])
    halo.send_corners()

    fill_patches(frame, s["pa"], 1, rows, 1, width)
    halo.receive_sides(early=True)
    fix_patches(frame, s["pa"], range(1, rows + 1), width)

    def finish_two(r, value):
        s["pre_two"][r] = value
        act = jnp.maximum(value, 0.0).astype(BF)
        s["act_two"][r] = act
        s["act_turned"][r] = turned(act)

    convolve(s["pa"], s["w_two"], 2, (rows - 4) // 2, 2, width, finish_two)

    for copy in loads[3:]:
        copy.wait()
    hw_rows, hw_cols = s["hw_rows"], s["hw_cols"]
    s["loss_acc"][...] = jnp.zeros_like(s["loss_acc"])
    last_halo = Halo(2, place, s)

    def prepare_head(k):
        for b in range(bins):
            tile = hw_all[b, k]
            start = k * total + b * bin_width
            hw_cols[:, pl.ds(pl.multiple_of(start, 128), bin_width)] = tile
            hw_rows[k, b * bin_width : (b + 1) * bin_width, :] = turned(tile)

    def head_unit(k, pair):
        eight = lax.broadcasted_iota(jnp.int32, (8, width), 0)
        group = lax.broadcasted_iota(jnp.int32, (total // 8, 8, width), 0)
        loss = s["loss_acc"][...]
        logits = [dot(hw_rows[k], s["act_turned"][r]).reshape(total // 8, 8, width) for r in pair]
        for r, value in zip(pair, logits):
            highest = jnp.max(jnp.max(value, axis=0), axis=0, keepdims=True)
            raised = jnp.exp(value - highest[None])
            summed = jnp.sum(jnp.sum(raised, axis=0), axis=0, keepdims=True)
            label = s["tg"][k, pl.ds(r, 1), :] - eight
            chosen = group * 8 == label[None]
            picked = jnp.sum(jnp.sum(jnp.where(chosen, value, 0.0), axis=0), axis=0, keepdims=True)
            loss = loss + (highest + jnp.log(summed) - picked)
            prob = raised * (scale / summed)[None]
            grad = jnp.where(chosen, prob - scale, prob).reshape(total, width).astype(BF)
            s["head_grad"][r, k] = grad
        s["loss_acc"][...] = loss

    def head_row(r):
        eight = lax.broadcasted_iota(jnp.int32, (8, width), 0)
        group = lax.broadcasted_iota(jnp.int32, (total // 8, 8, width), 0)
        loss = s["loss_acc"][...]
        back = jnp.zeros((channels, width), F32)
        for k in range(heads):
            value = dot(hw_rows[k], s["act_turned"][r]).reshape(total // 8, 8, width)
            highest = jnp.max(jnp.max(value, axis=0), axis=0, keepdims=True)
            raised = jnp.exp(value - highest[None])
            summed = jnp.sum(jnp.sum(raised, axis=0), axis=0, keepdims=True)
            label = s["tg"][k, pl.ds(r, 1), :] - eight
            chosen = group * 8 == label[None]
            picked = jnp.sum(jnp.sum(jnp.where(chosen, value, 0.0), axis=0), axis=0, keepdims=True)
            loss = loss + (highest + jnp.log(summed) - picked)
            prob = raised * (scale / summed)[None]
            grad = jnp.where(chosen, prob - scale, prob).reshape(total, width).astype(BF)
            s["head_grad"][r, k] = grad
            back = back + dot(hw_cols[:, k * total : (k + 1) * total], grad)
        s["loss_acc"][...] = loss
        finish_heads(r, back)

    def finish_heads(r, back):
        hidden = jnp.where(s["pre_two"][r] > 0, jnp.transpose(back), 0.0).astype(BF)
        s["back_two"][r + 1] = hidden
        frame[halo.line(r), :] = hidden.astype(F32)

    def loop(count, body):
        lax.fori_loop(0, count, lambda i, carry: (body(i), carry)[1], 0)

    for kk in range(heads):
        k = (own_first + kk) % heads
        if kk < half_heads:
            forward_head(kk)
        else:
            for copy in forwards[kk - half_heads]:
                copy.wait()
        prepare_head(k)
        loop((rows - 4) // 2, lambda i: head_unit(k, (2 + 2 * i, 3 + 2 * i)))
    def finish_inner(r):
        grads = s["head_grad"][r].reshape(heads * total, width)
        finish_heads(r, dot(hw_cols[...], grads))

    loop(rows - 4, lambda i: finish_inner(2 + i))
    halo.receive_sides()
    fix_patches(frame, s["pa"], (1, rows), width)
    halo.receive_rest()
    fill_patches(frame, s["pa"], 0, 2, rows + 1, width)
    convolve(s["pa"], s["w_two"], 0, 2, rows - 2, width, finish_two)
    loop(2, lambda i: head_row((rows - 1) * i))
    last_halo.send_rows(s["back_two"].at[1], s["back_two"].at[rows])
    last_halo.send_corners()
    loop(2, lambda i: head_row(1 + (rows - 3) * i))
    last_halo.send_sides()
    halo = last_halo

    early = Reduce("early", place, s, heads=2 * bins)
    late = Reduce("late", place, s)
    qr = early.part.shape[-2]
    feats = s["act_two"][...].reshape(rows * width, channels)
    for k in range(heads):
        c, kk = divmod(k, half_heads)
        grads = jnp.concatenate([s["head_grad"][r, k] for r in range(rows)], axis=1)
        value = dot(grads, feats).reshape(bins, bin_width // qr, qr, channels)
        for b in range(bins):
            early.part[c, :, 2 * b + kk] = value[b].astype(BF)
    kernel_grad(s["pa"], s["back_two"], s["g_acc"], rows, width)
    pack_grad(s["g_acc"], early.part, channels, 2 * bins)
    loss = s["loss_acc"][...]
    lanes = loss[:, :128]
    for i in range(1, width // 128):
        lanes = lanes + loss[:, i * 128 : (i + 1) * 128]
    row = lax.broadcasted_iota(jnp.int32, (qr, 128), 0)
    loss_tile = joined(jnp.where(row == 0, lanes, 0.0)).astype(BF)
    for q in range(place.nq):
        early.part[1, q, 2 * bins + 4] = loss_tile
        late.part[1, q, 4] = jnp.zeros((qr, channels), BF)
    early.step0()

    fill_patches(frame, s["pg"], 1, rows, 1, width)
    halo.receive_sides()
    fix_patches(frame, s["pg"], range(1, rows + 1), width)
    halo.receive_rest()
    fill_patches(frame, s["pg"], 0, 2, rows + 1, width)

    def finish_back(r, value):
        s["back_one"][r + 1] = jnp.where(s["pre_one"][r] > 0, value, 0.0).astype(BF)

    convolve(s["pg"], s["w_flip"], 0, rows // 2, 2, width, finish_back)
    early.step1()
    kernel_grad(s["px"], s["back_one"], s["g_acc"], rows, width)
    pack_grad(s["g_acc"], late.part, channels)
    late.step0()
    late.step1()
    early.step2()
    late.step2()
    early.step3()
    late.step3()
    early.step4()
    early.step5()
    stores = [load(early.out, early_ref, s["store"].at[0])]
    late.step4()
    stores.append(load(late.out.at[place.core], late_ref.at[place.core], s["store"].at[1]))
    late.step5()
    other = 1 - place.core
    stores.append(load(late.out.at[other], late_ref.at[other], s["store"].at[2]))
    for copy in stores:
        copy.wait()


def unpack(count, late_hbm, early_hbm, loss_ref, g1_hbm, g2_hbm, gh_hbm, *scratch):
    late_in, early_in, g1, g2, gh, sems = scratch
    heads, channels, bin_width = gh.shape
    loads = [load(early_hbm, early_in, sems.at[0]), load(late_hbm, late_in, sems.at[1])]
    loads[0].wait()
    unpack_grad(early_in, g2, channels, 2)
    stores = [load(g2, g2_hbm, sems.at[2])]
    loads[1].wait()
    unpack_grad(late_in, g1, channels)
    stores.append(load(g1, g1_hbm, sems.at[3]))
    for k in range(heads):
        c, kk = divmod(k, heads // 2)
        gh[k] = jnp.transpose(early_in[c, :, kk].astype(F32).reshape(bin_width, channels))
    stores.append(load(gh, gh_hbm, sems.at[4]))
    whole = jnp.sum(early_in[1, 0, 6].astype(F32), axis=0, keepdims=True)
    loss_ref[...] = jnp.sum(whole, axis=1, keepdims=True) * (1.0 / count)
    for copy in stores:
        copy.wait()


def per_device(inputs, conv_one, conv_two, head_weight, targets):
    rows, width, channels = inputs.shape
    heads, _, bin_width = head_weight.shape
    lat, lon, bins = (lax.axis_size(a) for a in ("lat", "lon", "bin"))
    cells_all = rows * lat * bins * width * lon
    scratch = plan(lat, lon, bins, rows, width, channels, heads, bin_width)
    vmem = pl.BlockSpec(memory_space=pltpu.VMEM)
    hbm = pl.BlockSpec(memory_space=pl.ANY)
    parts = pl.pallas_call(
        functools.partial(kernel, (lat, lon, bins, cells_all), tuple(scratch)),
        out_shape=[
            jax.ShapeDtypeStruct(scratch[name + "_out"].shape, BF) for name in ("late", "early")
        ],
        in_specs=[hbm] * 5,
        out_specs=[hbm] * 2,
        scratch_shapes=list(scratch.values()),
        compiler_params=pltpu.CompilerParams(
            collective_id=0, has_side_effects=True, vmem_limit_bytes=60 << 20
        ),
    )(inputs, conv_one, conv_two, head_weight, targets)
    loss, g1, g2, gh = pl.pallas_call(
        functools.partial(unpack, heads * cells_all),
        out_shape=[
            jax.ShapeDtypeStruct((1, 1), F32),
            jax.ShapeDtypeStruct(conv_one.shape, F32),
            jax.ShapeDtypeStruct(conv_two.shape, F32),
            jax.ShapeDtypeStruct(head_weight.shape, F32),
        ],
        in_specs=[hbm] * 2,
        out_specs=[vmem] + [hbm] * 3,
        scratch_shapes=[
            pltpu.VMEM(scratch["late_out"].shape, BF),
            pltpu.VMEM(scratch["early_out"].shape, BF),
            pltpu.VMEM(conv_one.shape, F32),
            pltpu.VMEM(conv_two.shape, F32),
            pltpu.VMEM(head_weight.shape, F32),
            pltpu.SemaphoreType.DMA((5,)),
        ],
    )(*parts)
    return (loss.reshape(()), g1, g2, gh)


def solution(mesh):
    in_specs = (
        P(("lat", "bin"), "lon", None),
        P(),
        P(),
        P(None, None, "bin"),
        P(None, "lat", "lon"),
    )
    out_specs = (P(), P(), P(), P(None, None, "bin"))
    return jax.shard_map(
        per_device, mesh=mesh, in_specs=in_specs, out_specs=out_specs, check_vma=False
    )
```
